256 devices in a mesh: doc: 32 (over z, y_lo, core), head: 8 (over y_hi, x).
Axes of the slice: x: 4, y: 4 (y_hi: 2, y_lo: 2; y = y_hi * 2 + y_lo), z: 8, core: 2. Of those that a mesh axis runs over, the one named last changes fastest.
Arguments:
- queries: bfloat16 [16384, 4096], P('doc', 'head'), may hold values from -6 to 6
- local_keys: bfloat16 [16384, 4096], P('doc', 'head'), may hold values from -6 to 6
- local_values: bfloat16 [16384, 4096], P('doc', 'head'), may hold values from -6 to 6
- mem_keys: bfloat16 [32768, 4096], P('doc', 'head'), may hold values from -6 to 6
- mem_values: bfloat16 [32768, 4096], P('doc', 'head'), may hold values from -6 to 6
- offsets: int32 [32, 4], P('doc'), may hold values from 1 to 4
- mem_lengths: int32 [32], replicated, may hold values from 1 to 1024
- out_weight: bfloat16 [4096, 2048], P('head'), may hold values from -0.09375 to 0.09375
Outputs:
- mixed: bfloat16 [16384, 2048], P(('doc', 'head'))
The draws below stay inside these ranges and needn't reach their ends.
All inputs are finite; a program needn't handle non-finite values.
Results may differ from the reference program's by a relative error of at most 0.015.
Values may be sent and summed in bfloat16 or wider, within the bound.
No kernel may reach another device: no remote copies, remote signals or barrier semaphores. Data moves between devices by JAX's collectives and lax.ppermute only.
A program may use at most 128 MiB of HBM per device.

```python
import math
import jax
import jax.numpy as jnp
from jax import lax

HEADS = 32
DH = 128
OUT = 2048
SLOTS = 4
QUERIES = 512
MEM = 1024
DOCS = 32


def draw_queries(key, part):
    full_shape = (DOCS * QUERIES, HEADS * DH)
    drawn = jnp.clip(jax.random.normal(jax.random.fold_in(key, 21), full_shape, jnp.float32), -6.0, 6.0)
    return drawn.astype(jnp.bfloat16)


def draw_local_keys(key, part):
    full_shape = (DOCS * QUERIES, HEADS * DH)
    drawn = jnp.clip(jax.random.normal(jax.random.fold_in(key, 22), full_shape, jnp.float32), -6.0, 6.0)
    return drawn.astype(jnp.bfloat16)


def touch_ends(result, rng, low, top_value):
    spot = [jax.random.randint(jax.random.fold_in(rng, axis), (), 0, length) for axis, length in enumerate(result.shape)]
    main_axis = result.shape.index(max(result.shape))
    neighbour = spot[:main_axis] + [(spot[main_axis] + 1) % result.shape[main_axis]] + spot[main_axis + 1:]
    return result.at[tuple(spot)].set(low).at[tuple(neighbour)].set(top_value)


def levels(own_key, extent, split, least, top_value):
    loudness, own = 1.0, jax.random.fold_in(own_key, 6)
    for axis_at, blocks in split:
        draws = jnp.exp(jax.random.uniform(jax.random.fold_in(own, axis_at), (blocks,), jnp.float32, least / len(split), top_value / len(split)))
        loudness = loudness * jnp.repeat(draws, extent[axis_at] // blocks).reshape([-1 if axis == axis_at else 1 for axis in range(len(extent))])
    return loudness


def normal_values(own_key, extent, width, limit, shards=(), kind=jnp.bfloat16):
    values = jax.random.normal(own_key, extent, jnp.float32) * width
    if len(shards) > 0:
        values = levels(own_key, extent, shards, -0.22, 0.18) * values
    return jnp.clip(values, min=-limit, max=limit).astype(kind)


def setup_inputs(seed: int = 0) -> dict:
    keys = jax.random.split(jax.random.key(seed), 9)
    queries = draw_queries(jax.random.fold_in(keys[8], 71), 0)
    local_keys = draw_local_keys(jax.random.fold_in(keys[8], 71), 0)
    local_values = normal_values(keys[2], (DOCS * QUERIES, HEADS * DH), 1.0, 6.0, ((0, 32), (1, 8)))
    mem_keys = normal_values(keys[3], (DOCS * MEM, HEADS * DH), 1.0, 6.0, ((0, 32), (1, 8)))
    mem_values = normal_values(keys[4], (DOCS * MEM, HEADS * DH), 1.0, 6.0, ((0, 32), (1, 8)))
    offsets = touch_ends(jax.random.randint(keys[5], (DOCS, SLOTS), 1, SLOTS + 1), jax.random.fold_in(keys[5], 1), 1, SLOTS).astype(jnp.int32)
    mem_lengths = touch_ends(jax.random.randint(keys[6], (DOCS,), 1, MEM + 1), jax.random.fold_in(keys[6], 1), 1, MEM).astype(jnp.int32)
    out_weight = normal_values(keys[7], (HEADS * DH, OUT), (HEADS * DH) ** -0.5, 0.09375, ((0, 8),))
    return {"queries": queries, "local_keys": local_keys, "local_values": local_values, "mem_keys": mem_keys, "mem_values": mem_values, "offsets": offsets, "mem_lengths": mem_lengths, "out_weight": out_weight}


def reference(queries, local_keys, local_values, mem_keys, mem_values, offsets, mem_lengths, out_weight):
    feature_width = HEADS * DH
    score_scale = 1.0 / math.sqrt(DH)
    query_rows = queries.reshape(DOCS, QUERIES, HEADS, DH)
    key_rows = local_keys.reshape(DOCS, QUERIES, HEADS, DH)
    value_rows = local_values.reshape(DOCS, QUERIES, HEADS, DH)
    memory_keys = mem_keys.reshape(DOCS, MEM, HEADS, DH)
    memory_values = mem_values.reshape(DOCS, MEM, HEADS, DH)
    causal = jnp.arange(QUERIES)[:, None] >= jnp.arange(QUERIES)[None, :]
    memory_index = jnp.arange(MEM)

    def one_doc(document):
        source = ((document - offsets[document]) % DOCS).astype(jnp.int32)
        owners = jnp.concatenate([document[None].astype(jnp.int32), source]).astype(jnp.int32)
        all_keys = jnp.concatenate([key_rows[document], memory_keys[owners].reshape(-1, HEADS, DH)], axis=0)
        all_values = jnp.concatenate([value_rows[document], memory_values[owners].reshape(-1, HEADS, DH)], axis=0)
        live_rows = memory_index[None, :] < mem_lengths[owners][:, None]
        live_mask = jnp.concatenate([causal, jnp.broadcast_to(live_rows.reshape(1, -1), (QUERIES, (SLOTS + 1) * MEM))], axis=1)
        scores = jnp.einsum('qhd,khd->hqk', query_rows[document].astype(jnp.float32), all_keys.astype(jnp.float32)) * score_scale
        scores = jnp.where(live_mask[None], scores, -1e+30)
        row_max = lax.optimization_barrier(jnp.max(scores, axis=-1, keepdims=True))
        exponent = jnp.where(live_mask[None], jnp.exp(scores - row_max), 0.0)
        weights = (exponent / lax.optimization_barrier(jnp.sum(exponent, axis=-1, keepdims=True))).astype(jnp.bfloat16)
        head_out = jnp.einsum('hqk,khd->qhd', weights.astype(jnp.float32), all_values.astype(jnp.float32)).astype(jnp.bfloat16)
        return head_out.reshape(QUERIES, feature_width)
    attended = lax.map(one_doc, jnp.arange(DOCS).astype(jnp.int32)).reshape(DOCS * QUERIES, feature_width)
    return jnp.dot(attended, out_weight, preferred_element_type=jnp.float32).astype(jnp.bfloat16)
```

```python
import math

import jax
import jax.numpy as jnp
from jax import lax
from jax.experimental import pallas as pl
from jax.experimental.pallas import tpu as pltpu
from jax.sharding import Mesh
from jax.sharding import PartitionSpec as P

DH = 128
DOC = ("z", "yl", "core")
HEAD = ("yh", "x")
NEG = -1e30
KEY_CHUNK = 512
LOG2E = math.log2(math.e)


def shift(value, axis, steps):
    count = lax.axis_size(axis)
    return lax.ppermute(value, axis, [(i, (i + steps) % count) for i in range(count)])


def swap(value, axis):
    return lax.ppermute(value, axis, [(0, 1), (1, 0)])


def lanes(x, width):
    return jnp.concatenate([x] * (width // DH), axis=1)


def scores_of(q, k):
    s = lax.dot_general(q, k, (((1,), (1,)), ((), ())), preferred_element_type=jnp.float32)
    return s * (LOG2E / math.sqrt(DH))


def with_ones(v):
    return jnp.concatenate([v, jnp.ones(v.shape, v.dtype)], axis=1)


def absorb(s, v, m_ref, acc_ref, rows):
    m_old = m_ref[rows, :]
    m_new = jnp.maximum(m_old, jnp.max(s, axis=1, keepdims=True))
    p = jnp.exp2(s - lanes(m_new, s.shape[1])).astype(jnp.bfloat16)
    pv = jnp.dot(p, with_ones(v), preferred_element_type=jnp.float32)
    acc_ref[rows, :] = acc_ref[rows, :] * lanes(jnp.exp2(m_old - m_new), 2 * DH) + pv
    m_ref[rows, :] = m_new


def absorb_memory(q, k_ref, v_ref, length, log_count, m_ref, acc_ref, rows):
    for start in range(0, k_ref.shape[0], KEY_CHUNK):

        @pl.when(length > start)
        def _(start=start):
            s = scores_of(q, k_ref[start : start + KEY_CHUNK, :]) + log_count
            row = lax.broadcasted_iota(jnp.int32, (1, KEY_CHUNK), 1) + start
            s = jnp.where(row < length, s, NEG)
            absorb(s, v_ref[start : start + KEY_CHUNK, :], m_ref, acc_ref, rows)


def reset(m_ref, acc_ref):
    m_ref[...] = jnp.full(m_ref.shape, NEG, jnp.float32)
    acc_ref[...] = jnp.zeros(acc_ref.shape, jnp.float32)


def finish(o_ref, l_ref, m_ref, acc_ref):
    total = acc_ref[:, DH:]
    seen = total > 0
    safe = jnp.where(seen, total, 1.0)
    o_ref[...] = (acc_ref[:, :DH] / safe).astype(o_ref.dtype)
    level = jnp.where(seen, m_ref[...] + jnp.log2(safe), NEG)
    l_ref[pl.ds(pl.program_id(0), 1), :] = level.T[:1, :]


def home_kernel(ints, q_ref, lk_ref, lv_ref, k_ref, v_ref, o_ref, l_ref, m_ref, acc_ref):
    reset(m_ref, acc_ref)
    block = q_ref.shape[0] // 2
    for r in range(2):
        rows = pl.ds(r * block, block)
        q = q_ref[rows, :]
        for c in range(r + 1):
            keys = pl.ds(c * block, block)
            s = scores_of(q, lk_ref[keys, :])
            if c == r:
                seen = lax.broadcasted_iota(jnp.int32, s.shape, 0) >= lax.broadcasted_iota(jnp.int32, s.shape, 1)
                s = jnp.where(seen, s, NEG)
            absorb(s, lv_ref[keys, :], m_ref, acc_ref, rows)
        absorb_memory(q, k_ref, v_ref, ints[0], 0.0, m_ref, acc_ref, rows)
    finish(o_ref, l_ref, m_ref, acc_ref)


def guest_kernel(ints, floats, q_ref, k0_ref, v0_ref, k1_ref, v1_ref, o_ref, l_ref, m_ref, acc_ref):
    reset(m_ref, acc_ref)
    rows = pl.ds(0, q_ref.shape[0])
    q = q_ref[...]
    absorb_memory(q, k0_ref, v0_ref, ints[0], floats[0], m_ref, acc_ref, rows)
    absorb_memory(q, k1_ref, v1_ref, ints[1], floats[1], m_ref, acc_ref, rows)
    finish(o_ref, l_ref, m_ref, acc_ref)


def merge_kernel(half, o0, l0, o1, l1, o2, l2, o3, l3, out_ref):
    levels = [l[...] for l in (l0, l1, l2, l3)]
    top = jnp.maximum(jnp.maximum(levels[0], levels[1]), jnp.maximum(levels[2], levels[3]))
    shares = [jnp.exp2(level - top) for level in levels]
    total = shares[0] + shares[1] + shares[2] + shares[3]
    shares = [share / total for share in shares]
    rows = shares[0].shape[0]
    packed = jnp.concatenate(shares + [jnp.zeros((DH - 4 * rows, shares[0].shape[1]), jnp.float32)], axis=0).T
    for h in range(out_ref.shape[1] // DH):
        cols = slice(h * DH, (h + 1) * DH)
        mixed = 0.0
        for i, o in enumerate((o0, o1, o2, o3)):
            lane = i * rows + h
            mixed = mixed + packed[:, lane : lane + 1] * o[:, cols].astype(jnp.float32)
        out_ref[:, cols] = mixed.astype(out_ref.dtype)


def project_kernel(where, a_ref, own, left_a, left_b, right_a, right_b, far_a, far_b, add_ref, out_ref, w_ref, sems, *, add):
    count = a_ref.shape[0]
    x, core = where[0], where[1]
    half = left_a.shape[1]
    mine = pl.ds(pl.multiple_of(core * half, half), half)
    theirs = pl.ds(pl.multiple_of((1 - core) * half, half), half)
    every = pl.ds(0, own.shape[0])
    left, right, far = (x + count - 1) % count, (x + 1) % count, (x + 2) % count
    del add
    pieces = [
        (own, x, every, pl.ds(0, 2 * half)),
        (left_a, left, every, mine),
        (left_b, left, every, theirs),
        (right_a, right, every, mine),
        (right_b, right, every, theirs),
        (far_a, far, every, mine),
        (far_b, far, every, theirs),
    ]
    copies = [
        pltpu.make_async_copy(src, w_ref.at[n, rows, cols], sems.at[n2])
        for n2, (src, (n, rows, cols)) in enumerate(
            (piece[0], ((0, 1, 1, 2, 2, 3, 3)[j], piece[2], piece[3])) for j, piece in enumerate(pieces)
        )
    ]
    for copy in copies:
        copy.start()
    acc = jnp.zeros(out_ref.shape, jnp.float32)
    for n, (index, waits) in enumerate(((x, (0,)), (left, (1, 2)), (right, (3, 4)), (far, (5, 6)))):
        for w in waits:
            copies[w].wait()
        acc = acc + jnp.dot(a_ref[index], w_ref[n], preferred_element_type=jnp.float32)
    if add_ref is not None:
        acc = acc + add_ref[...].astype(jnp.float32)
    out_ref[...] = acc.astype(out_ref.dtype)


def whole(shape, space=None):
    return pl.BlockSpec(shape, lambda *_: (0,) * len(shape)) if space is None else pl.BlockSpec(memory_space=space)


def by_head(rows):
    return pl.BlockSpec((rows, DH), lambda h, *_: (0, h))


def partial_attention(kernel, scalars, q, arrays, out_type, name):
    rows, width = q.shape
    heads = width // DH
    return pl.pallas_call(
        kernel,
        grid_spec=pltpu.PrefetchScalarGridSpec(
            num_scalar_prefetch=len(scalars),
            grid=(heads,),
            in_specs=[by_head(a.shape[0]) for a in (q, *arrays)],
            out_specs=[by_head(rows), whole((8, rows))],
            scratch_shapes=[pltpu.VMEM((rows, DH), jnp.float32), pltpu.VMEM((rows, 2 * DH), jnp.float32)],
        ),
        out_shape=[jax.ShapeDtypeStruct((rows, width), out_type), jax.ShapeDtypeStruct((8, rows), jnp.float32)],
        name=name,
    )(*scalars, q, *arrays)


def merge(half, home, others):
    rows, width = others[0][0].shape
    specs = [
        pl.BlockSpec((rows, width), lambda i, s: (s[0], 0)),
        pl.BlockSpec((8, rows), lambda i, s: (0, s[0])),
    ]
    for _ in others:
        specs += [whole((rows, width)), whole((8, rows))]
    return pl.pallas_call(
        merge_kernel,
        grid_spec=pltpu.PrefetchScalarGridSpec(
            num_scalar_prefetch=1, grid=(1,), in_specs=specs, out_specs=whole((rows, width))
        ),
        out_shape=jax.ShapeDtypeStruct((rows, width), jnp.bfloat16),
        name="merge",
    )(half, *home, *(a for pair in others for a in pair))


def project(where, gathered, weights, extra, name):
    count, rows, depth = gathered.shape
    width = weights[0].shape[1]
    specs = [whole(gathered.shape)] + [whole(None, pl.ANY)] * len(weights)
    args = [gathered, *weights]
    if extra is None:

        def kernel(where, a, *rest):
            project_kernel(where, a, *rest[:7], None, *rest[7:], add=False)
    else:
        specs.append(whole((rows, width)))
        args.append(extra)

        def kernel(where, a, *rest):
            project_kernel(where, a, *rest, add=True)

    return pl.pallas_call(
        kernel,
        grid_spec=pltpu.PrefetchScalarGridSpec(
            num_scalar_prefetch=1,
            grid=(1,),
            in_specs=specs,
            out_specs=whole((rows, width)),
            scratch_shapes=[pltpu.VMEM((count, depth, width), jnp.bfloat16), pltpu.SemaphoreType.DMA((7,))],
        ),
        out_shape=jax.ShapeDtypeStruct((rows, width), jnp.bfloat16),
        name=name,
    )(where, *args)


def per_device(queries, local_keys, local_values, mem_keys, mem_values, offsets, mem_lengths, out_weight):
    core = lax.axis_index("core")
    lane = lax.axis_index("yl")
    yh = lax.axis_index("yh")
    x = lax.axis_index("x")
    document = lax.axis_index(DOC)
    rows = queries.shape[0] // 2
    width = out_weight.shape[1]

    halves = [1 - yh, yh]
    parts = [lax.dynamic_slice_in_dim(queries, half * rows, rows, 0) for half in halves]
    far_offsets = shift(offsets, DOC, -4)
    near_offsets = shift(offsets, DOC, -2)
    far_q, near_q = [], []
    for part in parts:
        far_q.append(shift(part, DOC, -4))
    other_keys = swap(mem_keys, "core")
    other_values = swap(mem_values, "core")
    for part, far in zip(parts, far_q):
        near_q.append(swap(jnp.where(lane == 1, part, far), "yl"))

    half_width = width // 2
    mine = lax.dynamic_slice_in_dim(out_weight, core * half_width, half_width, 1)
    depth = mine.shape[0] // 2
    left = shift(mine, "x", 1)
    right = shift(mine, "x", -1)
    beyond = jnp.concatenate([shift(left[:depth], "x", 1), shift(right[depth:], "x", -1)], axis=0)
    weights = [out_weight, left, swap(left, "core"), right, swap(right, "core"), beyond, swap(beyond, "core")]

    own_length = mem_lengths[document]
    other_length = mem_lengths[document + 1 - 2 * core]

    def scalars(table, own, other):
        counts = jnp.stack([jnp.sum(table == own), jnp.sum(table == other)])
        lengths = jnp.stack([own_length, other_length])
        ints = jnp.where(counts > 0, lengths, 0).astype(jnp.int32)
        return ints, jnp.log2(jnp.maximum(counts, 1).astype(jnp.float32))

    memory = (mem_keys, mem_values, other_keys, other_values)
    home = partial_attention(
        home_kernel, (own_length[None],), queries, (local_keys, local_values, mem_keys, mem_values), jnp.float32, "home"
    )
    far_s = scalars(far_offsets, 4, 3 + 2 * core)
    near_s = scalars(near_offsets, 2, 1 + 2 * core)
    own_s = scalars(offsets, 0, 2 * core - 1)
    results = []
    for i in range(2):
        far = partial_attention(guest_kernel, far_s, far_q[i], memory, jnp.bfloat16, "far")
        near = partial_attention(guest_kernel, near_s, near_q[i], memory, jnp.bfloat16, "near")
        results.append(([shift(a, DOC, 4) for a in far], [shift(a, DOC, 2) for a in near]))
    own = [partial_attention(guest_kernel, own_s, part, memory, jnp.bfloat16, "own") for part in parts]

    where = jnp.stack([x, core]).astype(jnp.int32)
    count = lax.axis_size("x")
    gathered = []
    for i in range(2):
        far, near = results[i]
        attended = merge(halves[i][None].astype(jnp.int32), home, (own[i], far, near))
        tiles = attended.reshape(count, rows // count, attended.shape[1])
        gathered.append(lax.all_to_all(tiles, "x", 0, 0))
    given = project(where, gathered[0], weights, None, "give")
    taken = swap(given, "yh")
    return project(where, gathered[1], weights, taken, "keep")


def solution(mesh):
    split = Mesh(mesh.devices.reshape(-1, 2, 2, 2, 4), (*DOC, *HEAD))
    placed = (
        P(DOC, HEAD),
        P(DOC, HEAD),
        P(DOC, HEAD),
        P(DOC, HEAD),
        P(DOC, HEAD),
        P(DOC, None),
        P(),
        P(HEAD, None),
    )
    return jax.shard_map(
        per_device, mesh=split, in_specs=placed, out_specs=P((*DOC, *HEAD), None), check_vma=False
    )
```

```python
import math

import jax
import jax.numpy as jnp
from jax import lax
from jax.experimental import pallas as pl
from jax.experimental.pallas import tpu as pltpu
from jax.sharding import Mesh
from jax.sharding import PartitionSpec as P

DH = 128
DOC = ("z", "yl", "core")
HEAD = ("yh", "x")
NEG = -1e30
KEY_CHUNK = 512
TAIL = 16
SCALE = math.log2(math.e) / math.sqrt(DH)


def shift(value, axis, steps):
    count = lax.axis_size(axis)
    return lax.ppermute(value, axis, [(i, (i + steps) % count) for i in range(count)])


def swap(value, axis):
    return lax.ppermute(value, axis, [(0, 1), (1, 0)])


def part_ways(value):
    count = lax.axis_size("x")
    up = [(i, (i + 1) % count) for i in range(count)]
    down = [(count + i, count + (i - 1) % count) for i in range(count)]
    return lax.ppermute(value, ("core", "x"), up + down)


def lanes(x, width):
    return jnp.concatenate([x] * (width // DH), axis=1)


def scores_of(q, k):
    return lax.dot_general(q, k, (((1,), (1,)), ((), ())), preferred_element_type=jnp.float32) * SCALE


def with_ones(v):
    return jnp.concatenate([v, jnp.ones(v.shape, v.dtype)], axis=1)


def absorb(s, v, m_ref, acc_ref):
    m_old = m_ref[...]
    m_new = jnp.maximum(m_old, jnp.max(s, axis=1, keepdims=True))
    p = jnp.exp2(s - lanes(m_new, s.shape[1])).astype(jnp.bfloat16)
    pv = jnp.dot(p, with_ones(v), preferred_element_type=jnp.float32)
    acc_ref[...] = acc_ref[...] * lanes(jnp.exp2(m_old - m_new), 2 * DH) + pv
    m_ref[...] = m_new


def reset(m_ref, acc_ref):
    m_ref[...] = jnp.full(m_ref.shape, NEG, jnp.float32)
    acc_ref[...] = jnp.zeros(acc_ref.shape, jnp.float32)


def log2_count(count):
    return jnp.where(count >= 4, 2.0, jnp.where(count >= 3, math.log2(3), jnp.where(count >= 2, 1.0, 0.0)))


class Memory:
    def __init__(self, keys, values, buffers, sems, length, count):
        self.keys, self.values, self.buffers, self.sems = keys, values, buffers, sems
        self.length, self.bias = jnp.where(count > 0, length, 0), log2_count(count)
        self.chunks = range(0, keys.shape[0], KEY_CHUNK)

    def copies(self, h, j):
        rows, cols = pl.ds(self.chunks[j], KEY_CHUNK), pl.ds(pl.multiple_of(h * DH, DH), DH)
        return [
            pltpu.make_async_copy(src.at[rows, cols], self.buffers.at[i, h, rows, :], self.sems.at[i, h, j])
            for i, src in enumerate((self.keys, self.values))
        ]

    def fetch(self, h):
        for j, start in enumerate(self.chunks):

            @pl.when(self.length > start)
            def _(j=j):
                for copy in self.copies(h, j):
                    copy.start()

    def use(self, h, q, m_ref, acc_ref):
        for j, start in enumerate(self.chunks):

            @pl.when(self.length > start)
            def _(j=j, start=start):
                for copy in self.copies(h, j):
                    copy.wait()
                row = lax.broadcasted_iota(jnp.int32, (1, KEY_CHUNK), 1) + start
                bias = jnp.where(row < self.length, self.bias, NEG)
                rows = pl.ds(start, KEY_CHUNK)
                absorb(scores_of(q, self.buffers[0, h, rows, :]) + bias, self.buffers[1, h, rows, :], m_ref, acc_ref)


def finish(h, rows, put, level_ref, m_ref, acc_ref):
    total = acc_ref[:, DH:]
    seen = total > 0
    safe = jnp.where(seen, total, 1.0)
    put((acc_ref[:, :DH] / safe).astype(jnp.bfloat16))
    rest = jnp.where(seen, m_ref[...] + jnp.log2(safe), NEG).T[:1, :]
    for i in range(3):
        term = rest.astype(jnp.bfloat16).astype(jnp.float32)
        level_ref[pl.ds(3 * h + i, 1), :rows] = term
        rest = rest - term


def home_kernel(offsets, lengths, q_ref, lk_ref, lv_ref, *refs, partner):
    k0, v0, k1, v1, out_ref, m_ref, acc_ref, level_ref, buf0, buf1, sem0, sem1 = refs
    heads = q_ref.shape[1] // DH
    core, document, yh = lax.axis_index("core"), lax.axis_index(DOC), lax.axis_index("yh")
    rows = q_ref.shape[0] // 2
    first = (1 - yh if partner else yh) * rows
    count = sum(jnp.where((offsets[0, i] == 1) & (core == 1), 1, 0) for i in range(offsets.shape[1]))
    memories = [
        Memory(k0, v0, buf0, sem0, lengths[document], jnp.int32(1)),
        Memory(k1, v1, buf1, sem1, lengths[document + 1 - 2 * core], count),
    ]
    for h in range(heads):
        for memory in memories:
            memory.fetch(h)
    level_ref[...] = jnp.zeros(level_ref.shape, jnp.float32)

    def one_head(h, carry):
        cols = pl.ds(pl.multiple_of(h * DH, DH), DH)
        reset(m_ref, acc_ref)
        q = q_ref[pl.ds(pl.multiple_of(first, rows), rows), cols]
        s = scores_of(q, lk_ref[:, cols])
        row = lax.broadcasted_iota(jnp.int32, s.shape, 0) + first
        s = jnp.where(row >= lax.broadcasted_iota(jnp.int32, s.shape, 1), s, NEG)
        absorb(s, lv_ref[:, cols], m_ref, acc_ref)
        for memory in memories:
            memory.use(h, q, m_ref, acc_ref)

        def put(o):
            out_ref[pl.ds(0, rows), cols] = o

        finish(h, rows, put, level_ref, m_ref, acc_ref)
        return carry

    lax.fori_loop(0, heads, one_head, 0)
    out_ref[pl.ds(rows, TAIL), :] = level_ref[...].astype(jnp.bfloat16)


def guest_kernel(lengths, q_ref, k0, v0, k1, v1, out_ref, m_ref, acc_ref, level_ref, buf0, buf1, sem0, sem1, *, back):
    heads, rows = q_ref.shape[1] // DH, q_ref.shape[0] - TAIL
    core, document = lax.axis_index("core"), lax.axis_index(DOC)
    table = q_ref[pl.ds(rows, TAIL), pl.ds(0, DH)].astype(jnp.float32)
    own = jnp.sum(jnp.where(table == back, 1.0, 0.0)).astype(jnp.int32)
    wanted = (back - 1 + 2 * core).astype(jnp.float32)
    other = jnp.sum(jnp.where(table == wanted, 1.0, 0.0)).astype(jnp.int32)
    memories = [
        Memory(k0, v0, buf0, sem0, lengths[document], own),
        Memory(k1, v1, buf1, sem1, lengths[document + 1 - 2 * core], other),
    ]
    for h in range(heads):
        for memory in memories:
            memory.fetch(h)
    level_ref[...] = jnp.zeros(level_ref.shape, jnp.float32)

    def one_head(h, carry):
        cols = pl.ds(pl.multiple_of(h * DH, DH), DH)
        reset(m_ref, acc_ref)
        q = q_ref[pl.ds(0, rows), cols]
        for memory in memories:
            memory.use(h, q, m_ref, acc_ref)

        def put(o):
            out_ref[pl.ds(0, rows), cols] = o

        finish(h, rows, put, level_ref, m_ref, acc_ref)
        return carry

    lax.fori_loop(0, heads, one_head, 0)
    out_ref[pl.ds(rows, TAIL), :] = level_ref[...].astype(jnp.bfloat16)


def whole(shape):
    return pl.BlockSpec(shape, lambda *_: (0,) * len(shape))


def anywhere():
    return pl.BlockSpec(memory_space=pl.ANY)


def attention(kernel, scalars, blocks, memory, rows, out_shape):
    heads = blocks[0].shape[1] // DH
    mem_rows, width = memory[0].shape
    buffer = pltpu.VMEM((2, heads, mem_rows, DH), jnp.bfloat16)
    sems = pltpu.SemaphoreType.DMA((2, heads, mem_rows // KEY_CHUNK))
    return pl.pallas_call(
        kernel,
        grid_spec=pltpu.PrefetchScalarGridSpec(
            num_scalar_prefetch=len(scalars),
            grid=(1,),
            in_specs=[whole(a.shape) for a in blocks] + [anywhere()] * 4,
            out_specs=whole(out_shape),
            scratch_shapes=[
                pltpu.VMEM((rows, DH), jnp.float32),
                pltpu.VMEM((rows, 2 * DH), jnp.float32),
                pltpu.VMEM((TAIL, width), jnp.float32),
                buffer,
                buffer,
                sems,
                sems,
            ],
        ),
        out_shape=jax.ShapeDtypeStruct(out_shape, jnp.bfloat16),
    )(*scalars, *blocks, *memory)


def merge_kernel(home_ref, far_ref, near_ref, out_ref, share_ref):
    rows, width = out_ref.shape
    heads = width // DH
    parts = [home_ref[...], far_ref[...], near_ref[...]]
    tails = [part[rows:, :rows].astype(jnp.float32) for part in parts]
    for h in range(heads):
        levels = [tail[3 * h : 3 * h + 1] + tail[3 * h + 1 : 3 * h + 2] + tail[3 * h + 2 : 3 * h + 3] for tail in tails]
        top = jnp.maximum(jnp.maximum(levels[0], levels[1]), levels[2])
        shares = [jnp.exp2(level - top) for level in levels]
        total = shares[0] + shares[1] + shares[2]
        for i, share in enumerate(shares):
            share_ref[pl.ds(3 * h + i, 1), :] = share / total
    columns = share_ref[...].T
    for h in range(heads):
        cols = slice(h * DH, (h + 1) * DH)
        mixed = sum(columns[:, 3 * h + i : 3 * h + i + 1] * part[:rows, cols].astype(jnp.float32) for i, part in enumerate(parts))
        out_ref[:, cols] = mixed.astype(out_ref.dtype)


def merge(home, far, near):
    rows, width = far.shape[0] - TAIL, far.shape[1]
    return pl.pallas_call(
        merge_kernel,
        grid=(1,),
        in_specs=[whole(home.shape), whole(far.shape), whole(near.shape)],
        out_specs=whole((rows, width)),
        out_shape=jax.ShapeDtypeStruct((rows, width), jnp.bfloat16),
        scratch_shapes=[pltpu.VMEM((DH, rows), jnp.float32)],
        name="merge",
    )(home, far, near)


def project_kernel(a_ref, own, near, near_other, far, far_other, *rest):
    *extra, out_ref, w_ref, sems = rest
    count, depth = a_ref.shape[0], own.shape[0]
    half = depth // 2
    x, core = lax.axis_index("x"), lax.axis_index("core")
    side = (x + count - 1 + 2 * core) % count
    other_side = (x + 1 + count - 2 * core) % count
    opposite = (x + 2) % count
    copies = []
    for n, src in enumerate((own, near, near_other)):
        for i in range(2):
            rows = pl.ds(i * half, half)
            copies.append((src.at[rows, :], w_ref.at[2 * n + i]))
    copies.append((far, w_ref.at[6 + core]))
    copies.append((far_other, w_ref.at[7 - core]))
    copies = [pltpu.make_async_copy(src, dst, sems.at[i]) for i, (src, dst) in enumerate(copies)]
    for copy in copies:
        copy.start()
    acc = jnp.zeros(out_ref.shape, jnp.float32)
    for n, index in enumerate((x, side, other_side, opposite)):
        for i in range(2):
            if n < 3:
                copies[2 * n + i].wait()
            elif i == 0:
                copies[6].wait()
                copies[7].wait()
            a = a_ref[index, :, i * half : (i + 1) * half]
            acc = acc + jnp.dot(a, w_ref[2 * n + i], preferred_element_type=jnp.float32)
    for ref in extra:
        acc = acc + ref[...].astype(jnp.float32)
    out_ref[...] = acc.astype(out_ref.dtype)


def project(gathered, weights, extra):
    count, rows, depth = gathered.shape
    width = weights[0].shape[1]
    return pl.pallas_call(
        project_kernel,
        grid=(1,),
        in_specs=[whole(gathered.shape)] + [anywhere()] * len(weights) + [whole(e.shape) for e in extra],
        out_specs=whole((rows, width)),
        scratch_shapes=[pltpu.VMEM((2 * count, depth // 2, width), jnp.bfloat16), pltpu.SemaphoreType.DMA((8,))],
        out_shape=jax.ShapeDtypeStruct((rows, width), jnp.bfloat16),
    )(gathered, *weights, *extra)


def after(value, *others):
    return lax.optimization_barrier((value, *others))[0]


def step(queries, local_keys, local_values, mem_keys, mem_values, offsets, mem_lengths, out_weight):
    core = lax.axis_index("core")
    yh = lax.axis_index("yh")
    rows = queries.shape[0] // 2
    width = queries.shape[1]

    tail = jnp.pad(offsets.astype(jnp.bfloat16), ((0, TAIL - 1), (0, width - offsets.shape[1])))
    loads = [
        jnp.concatenate([lax.dynamic_slice_in_dim(queries, half * rows, rows, 0), tail], axis=0) for half in (1 - yh, yh)
    ]
    guests = [[shift(load, DOC, -back) for back in (4, 2)] for load in loads]
    other = [swap(a, "core") for a in (mem_keys, mem_values)]
    memory = (mem_keys, mem_values, *other)
    near = part_ways(after(out_weight, *loads))

    def at_home(queries, partner):
        def kernel(*refs):
            home_kernel(*refs, partner=partner)

        blocks = (queries, local_keys, local_values)
        return attention(kernel, (offsets, mem_lengths), blocks, memory, rows, (rows + TAIL, width))

    def guest(load, back):
        def kernel(*refs):
            guest_kernel(*refs, back=back)

        out = attention(kernel, (mem_lengths,), (load,), memory, rows, load.shape)
        return out, shift(out, DOC, back)

    home0 = at_home(queries, True)
    far0, from_far0 = guest(after(guests[0][0], home0), 4)
    near0, from_near0 = guest(after(guests[0][1], far0), 2)
    far1, from_far1 = guest(after(guests[1][0], near0), 4)
    near1, from_near1 = guest(after(guests[1][1], far1), 2)

    half_depth = out_weight.shape[0] // 2
    near = after(near, far1)
    far = part_ways(lax.dynamic_slice_in_dim(near, core * half_depth, half_depth, 0))
    weights = [out_weight, near, swap(near, "core"), far, swap(far, "core")]

    home1 = at_home(after(queries, near1), False)

    count = lax.axis_size("x")

    def attended(home, far, near):
        merged = merge(home, far, near)
        return lax.all_to_all(merged.reshape(count, rows // count, width), "x", 0, 0)

    given = project(attended(home0, from_far0, from_near0), weights, ())
    kept = attended(home1, from_far1, from_near1)
    return project(kept, weights, (swap(given, "yh"),))


def solution(mesh):
    split = Mesh(mesh.devices.reshape(-1, 2, 2, 2, 4), (*DOC, *HEAD))
    placed = (
        P(DOC, HEAD),
        P(DOC, HEAD),
        P(DOC, HEAD),
        P(DOC, HEAD),
        P(DOC, HEAD),
        P(DOC, None),
        P(),
        P(HEAD, None),
    )
    return jax.shard_map(step, mesh=split, in_specs=placed, out_specs=P((*DOC, *HEAD), None), check_vma=False)
```

```python
import math

import jax
import jax.numpy as jnp
from jax import lax
from jax.experimental import pallas as pl
from jax.experimental.pallas import tpu as pltpu
from jax.sharding import Mesh
from jax.sharding import PartitionSpec as P

DH = 128
DOC = ("z", "yl", "core")
HEAD = ("yh", "x")
NEG = -1e30
KEY_CHUNK = 512
TAIL = 16
SCALE = math.log2(math.e) / math.sqrt(DH)


def shift(value, axis, steps):
    count = lax.axis_size(axis)
    return lax.ppermute(value, axis, [(i, (i + steps) % count) for i in range(count)])


def swap(value, axis):
    return lax.ppermute(value, axis, [(0, 1), (1, 0)])


def part_ways(value):
    count = lax.axis_size("x")
    up = [(i, (i + 1) % count) for i in range(count)]
    down = [(count + i, count + (i - 1) % count) for i in range(count)]
    return lax.ppermute(value, ("core", "x"), up + down)


def lanes(x, width):
    return jnp.concatenate([x] * (width // DH), axis=1)


def scores_of(q, k):
    return lax.dot_general(q, k, (((1,), (1,)), ((), ())), preferred_element_type=jnp.float32) * SCALE


def with_ones(v):
    return jnp.concatenate([v, jnp.ones(v.shape, v.dtype)], axis=1)


def absorb(h, s, v, m_ref, acc_ref):
    m_old = m_ref[h]
    m_new = jnp.maximum(m_old, jnp.max(s, axis=1, keepdims=True))
    p = jnp.exp2(s - lanes(m_new, s.shape[1])).astype(jnp.bfloat16)
    pv = jnp.dot(p, with_ones(v), preferred_element_type=jnp.float32)
    acc_ref[h] = acc_ref[h] * lanes(jnp.exp2(m_old - m_new), 2 * DH) + pv
    m_ref[h] = m_new


def reset(m_ref, acc_ref):
    m_ref[...] = jnp.full(m_ref.shape, NEG, jnp.float32)
    acc_ref[...] = jnp.zeros(acc_ref.shape, jnp.float32)


def log2_count(count):
    return jnp.where(count >= 4, 2.0, jnp.where(count >= 3, math.log2(3), jnp.where(count >= 2, 1.0, 0.0)))


def of_head(h):
    return slice(h * DH, (h + 1) * DH)


def absorb_memories(arrays, lengths, counts, queries, buffer, sems, m_ref, acc_ref):
    per_document = arrays[0].shape[0] // KEY_CHUNK
    live = [jnp.where(count > 0, length, 0) for length, count in zip(lengths, counts)]
    biases = [log2_count(count) for count in counts]

    def copies(document, j, chunk):
        rows = pl.ds(j * KEY_CHUNK, KEY_CHUNK)
        return [
            pltpu.make_async_copy(arrays[2 * document + i].at[rows, :], buffer.at[chunk, i], sems.at[chunk, i])
            for i in range(2)
        ]

    for document in range(2):
        for j in range(per_document):

            @pl.when(live[document] > j * KEY_CHUNK)
            def _(document=document, j=j):
                for copy in copies(document, j, document * per_document + j):
                    copy.start()

    def fold(chunk, carry):
        second = chunk >= per_document
        left = jnp.where(second, live[1], live[0]) - jnp.where(second, chunk - per_document, chunk) * KEY_CHUNK

        @pl.when(left > 0)
        def _():
            for copy in copies(0, 0, chunk):
                copy.wait()
            row = lax.broadcasted_iota(jnp.int32, (1, KEY_CHUNK), 1)
            bias = jnp.where(row < left, jnp.where(second, biases[1], biases[0]), NEG)
            for h in range(m_ref.shape[0]):
                keys, values = (buffer[chunk, i, :, of_head(h)] for i in range(2))
                absorb(h, scores_of(queries(h), keys) + bias, values, m_ref, acc_ref)

        return carry

    lax.fori_loop(0, 2 * per_document, fold, 0)


def finish(out_ref, level_ref, m_ref, acc_ref):
    heads, rows = m_ref.shape[:2]
    level_ref[...] = jnp.zeros(level_ref.shape, jnp.float32)
    for h in range(heads):
        total = acc_ref[h, :, DH:]
        seen = total > 0
        safe = jnp.where(seen, total, 1.0)
        out_ref[:rows, of_head(h)] = (acc_ref[h, :, :DH] / safe).astype(jnp.bfloat16)
        rest = jnp.where(seen, m_ref[h] + jnp.log2(safe), NEG).T[:1, :]
        for i in range(3):
            term = rest.astype(jnp.bfloat16).astype(jnp.float32)
            level_ref[3 * h + i : 3 * h + i + 1, :rows] = term
            rest = rest - term
    out_ref[rows:, :] = level_ref[...].astype(jnp.bfloat16)


def home_kernel(offsets, lengths, q_ref, lk_ref, lv_ref, *refs, partner):
    *arrays, out_ref, m_ref, acc_ref, level_ref, buffer, sems = refs
    core, document, yh = lax.axis_index("core"), lax.axis_index(DOC), lax.axis_index("yh")
    heads, rows = m_ref.shape[:2]
    first = (1 - yh if partner else yh) * rows
    count = sum(jnp.where((offsets[0, i] == 1) & (core == 1), 1, 0) for i in range(offsets.shape[1]))
    reset(m_ref, acc_ref)

    def queries(h):
        return q_ref[pl.ds(pl.multiple_of(first, rows), rows), of_head(h)]

    shape = (rows, lk_ref.shape[0])
    seen = lax.broadcasted_iota(jnp.int32, shape, 0) + first >= lax.broadcasted_iota(jnp.int32, shape, 1)
    for h in range(heads):
        s = jnp.where(seen, scores_of(queries(h), lk_ref[:, of_head(h)]), NEG)
        absorb(h, s, lv_ref[:, of_head(h)], m_ref, acc_ref)
    live = lengths[document], lengths[document + 1 - 2 * core]
    absorb_memories(arrays, live, (jnp.int32(1), count), queries, buffer, sems, m_ref, acc_ref)
    finish(out_ref, level_ref, m_ref, acc_ref)


def guest_kernel(lengths, q_ref, *refs, back):
    *arrays, out_ref, m_ref, acc_ref, level_ref, buffer, sems = refs
    rows = m_ref.shape[1]
    core, document = lax.axis_index("core"), lax.axis_index(DOC)
    table = q_ref[rows:, :DH].astype(jnp.float32)
    own = jnp.sum(jnp.where(table == back, 1.0, 0.0)).astype(jnp.int32)
    wanted = (back - 1 + 2 * core).astype(jnp.float32)
    other = jnp.sum(jnp.where(table == wanted, 1.0, 0.0)).astype(jnp.int32)
    reset(m_ref, acc_ref)
    live = lengths[document], lengths[document + 1 - 2 * core]
    absorb_memories(
        arrays, live, (own, other), lambda h: q_ref[:rows, of_head(h)], buffer, sems, m_ref, acc_ref
    )
    finish(out_ref, level_ref, m_ref, acc_ref)


def pack_kernel(offsets, q_ref, *out_refs):
    yh = lax.axis_index("yh")
    rows, width = q_ref.shape[0] // 2, q_ref.shape[1]
    lane = lax.broadcasted_iota(jnp.int32, (TAIL, width), 1)
    top = lax.broadcasted_iota(jnp.int32, (TAIL, width), 0) == 0
    tail = jnp.zeros((TAIL, width), jnp.float32)
    for i in range(offsets.shape[1]):
        tail = jnp.where(top & (lane == i), offsets[0, i].astype(jnp.float32), tail)
    for half, out_ref in zip((1 - yh, yh), out_refs):
        out_ref[:rows, :] = q_ref[pl.ds(pl.multiple_of(half * rows, rows), rows), :]
        out_ref[rows:, :] = tail.astype(jnp.bfloat16)


def whole(shape):
    return pl.BlockSpec(shape, lambda *_: (0,) * len(shape))


def anywhere():
    return pl.BlockSpec(memory_space=pl.ANY)


def pack(queries, offsets):
    rows, width = queries.shape[0] // 2 + TAIL, queries.shape[1]
    return pl.pallas_call(
        pack_kernel,
        grid_spec=pltpu.PrefetchScalarGridSpec(
            num_scalar_prefetch=1, grid=(1,), in_specs=[whole(queries.shape)], out_specs=[whole((rows, width))] * 2
        ),
        out_shape=[jax.ShapeDtypeStruct((rows, width), jnp.bfloat16)] * 2,
        name="pack",
    )(offsets, queries)


def attention(kernel, scalars, blocks, memory, rows):
    mem_rows, width = memory[0].shape
    heads = width // DH
    chunks = 2 * mem_rows // KEY_CHUNK
    return pl.pallas_call(
        kernel,
        grid_spec=pltpu.PrefetchScalarGridSpec(
            num_scalar_prefetch=len(scalars),
            grid=(1,),
            in_specs=[whole(a.shape) for a in blocks] + [anywhere()] * 4,
            out_specs=whole((rows + TAIL, width)),
            scratch_shapes=[
                pltpu.VMEM((heads, rows, DH), jnp.float32),
                pltpu.VMEM((heads, rows, 2 * DH), jnp.float32),
                pltpu.VMEM((TAIL, width), jnp.float32),
                pltpu.VMEM((chunks, 2, KEY_CHUNK, width), jnp.bfloat16),
                pltpu.SemaphoreType.DMA((chunks, 2)),
            ],
        ),
        out_shape=jax.ShapeDtypeStruct((rows + TAIL, width), jnp.bfloat16),
    )(*scalars, *blocks, *memory)


def merge_kernel(home_ref, far_ref, near_ref, *refs):
    *tiles, share_ref, whole_ref = refs
    rows, width = whole_ref.shape
    heads, count = width // DH, len(tiles)
    parts = [home_ref, far_ref, near_ref]
    tails = [part[rows:, :rows].astype(jnp.float32) for part in parts]
    for h in range(heads):
        levels = [tail[3 * h : 3 * h + 1] + tail[3 * h + 1 : 3 * h + 2] + tail[3 * h + 2 : 3 * h + 3] for tail in tails]
        top = jnp.maximum(jnp.maximum(levels[0], levels[1]), levels[2])
        shares = [jnp.exp2(level - top) for level in levels]
        total = shares[0] + shares[1] + shares[2]
        for i, share in enumerate(shares):
            share_ref[3 * h + i : 3 * h + i + 1, :] = share / total
    columns = share_ref[...].T
    for h in range(heads):
        mixed = 0.0
        for i, part in enumerate(parts):
            mixed = mixed + columns[:, 3 * h + i : 3 * h + i + 1] * part[:rows, of_head(h)].astype(jnp.float32)
        whole_ref[:, of_head(h)] = mixed.astype(whole_ref.dtype)
    block = rows // count
    for k, tile in enumerate(tiles):
        place = (lax.axis_index("x") + k) % count
        tile[...] = whole_ref[pl.ds(pl.multiple_of(place * block, block), block), :]


def merge(home, far, near):
    rows, width = far.shape[0] - TAIL, far.shape[1]
    count = lax.axis_size("x")
    tile = (rows // count, width)
    return pl.pallas_call(
        merge_kernel,
        grid=(1,),
        in_specs=[whole(home.shape)] * 3,
        out_specs=[whole(tile)] * count,
        out_shape=[jax.ShapeDtypeStruct(tile, jnp.bfloat16)] * count,
        scratch_shapes=[pltpu.VMEM((DH, rows), jnp.float32), pltpu.VMEM((rows, width), jnp.bfloat16)],
        name="merge",
    )(home, far, near)


def project_kernel(*refs):
    mine, below, opposite, above, own, near, near_other, far, far_other, *extra, out_ref, w_ref, sems = refs
    half = own.shape[0] // 2
    core = lax.axis_index("core")
    copies = []
    for n, src in enumerate((own, near, near_other)):
        for i in range(2):
            copies.append((src.at[pl.ds(i * half, half), :], w_ref.at[2 * n + i]))
    copies.append((far, w_ref.at[6 + core]))
    copies.append((far_other, w_ref.at[7 - core]))
    copies = [pltpu.make_async_copy(src, dst, sems.at[i]) for i, (src, dst) in enumerate(copies)]
    for copy in copies:
        copy.start()
    side = jnp.where(core == 0, below[...], above[...])
    other_side = jnp.where(core == 0, above[...], below[...])
    acc = jnp.zeros(out_ref.shape, jnp.float32)
    for n, tile in enumerate((mine[...], side, other_side, opposite[...])):
        for i in range(2):
            if n < 3:
                copies[2 * n + i].wait()
            elif i == 0:
                copies[6].wait()
                copies[7].wait()
            a = tile[:, i * half : (i + 1) * half]
            acc = acc + jnp.dot(a, w_ref[2 * n + i], preferred_element_type=jnp.float32)
    for ref in extra:
        acc = acc + ref[...].astype(jnp.float32)
    out_ref[...] = acc.astype(out_ref.dtype)


def project(tiles, weights, extra):
    rows = tiles[0].shape[0]
    depth, width = weights[0].shape
    return pl.pallas_call(
        project_kernel,
        grid=(1,),
        in_specs=[whole(t.shape) for t in tiles] + [anywhere()] * len(weights) + [whole(e.shape) for e in extra],
        out_specs=whole((rows, width)),
        scratch_shapes=[pltpu.VMEM((2 * len(tiles), depth // 2, width), jnp.bfloat16), pltpu.SemaphoreType.DMA((8,))],
        out_shape=jax.ShapeDtypeStruct((rows, width), jnp.bfloat16),
    )(*tiles, *weights, *extra)


def after(value, *others):
    return lax.optimization_barrier((value, *others))[0]


def step(queries, local_keys, local_values, mem_keys, mem_values, offsets, mem_lengths, out_weight):
    core = lax.axis_index("core")
    rows = queries.shape[0] // 2

    loads = pack(queries, offsets)
    guests = [[shift(load, DOC, -back) for back in (4, 2)] for load in loads]
    other = [swap(a, "core") for a in (mem_keys, mem_values)]
    memory = (mem_keys, mem_values, *other)
    near = part_ways(after(out_weight, *loads))

    def at_home(queries, partner):
        def kernel(*refs):
            home_kernel(*refs, partner=partner)

        blocks = (queries, local_keys, local_values)
        return attention(kernel, (offsets, mem_lengths), blocks, memory, rows)

    def guest(load, back):
        def kernel(*refs):
            guest_kernel(*refs, back=back)

        out = attention(kernel, (mem_lengths,), (load,), memory, rows)
        return out, shift(out, DOC, back)

    home0 = at_home(queries, True)
    far0, from_far0 = guest(after(guests[0][0], home0), 4)
    near0, from_near0 = guest(after(guests[0][1], far0), 2)
    far1, from_far1 = guest(after(guests[1][0], near0), 4)
    near1, from_near1 = guest(after(guests[1][1], far1), 2)

    half_depth = out_weight.shape[0] // 2
    near = after(near, far1)
    far = part_ways(lax.dynamic_slice_in_dim(near, core * half_depth, half_depth, 0))
    weights = [out_weight, near, swap(near, "core"), far, swap(far, "core")]

    home1 = at_home(after(queries, near1), False)

    def attended(home, far, near):
        mine, *tiles = merge(home, far, near)
        return mine, *(shift(tile, "x", k) for k, tile in enumerate(tiles, 1))

    given = project(attended(home0, from_far0, from_near0), weights, ())
    kept = attended(home1, from_far1, from_near1)
    return project(kept, weights, (swap(given, "yh"),))


def solution(mesh):
    split = Mesh(mesh.devices.reshape(-1, 2, 2, 2, 4), (*DOC, *HEAD))
    placed = (
        P(DOC, HEAD),
        P(DOC, HEAD),
        P(DOC, HEAD),
        P(DOC, HEAD),
        P(DOC, HEAD),
        P(DOC, None),
        P(),
        P(HEAD, None),
    )
    return jax.shard_map(step, mesh=split, in_specs=placed, out_specs=P((*DOC, *HEAD), None), check_vma=False)
```

```python
import math

import jax
import jax.numpy as jnp
from jax import lax
from jax.experimental import pallas as pl
from jax.experimental.pallas import tpu as pltpu
from jax.sharding import Mesh
from jax.sharding import PartitionSpec as P

DH = 128
DOC = ("z", "yl", "core")
HEAD = ("yh", "x")
NEG = -1e30
KEY_CHUNK = 512
TAIL = 16
SCALE = math.log2(math.e) / math.sqrt(DH)

VMEM_LIMIT = 24 * 2**20


def shift(value, axis, steps):
    count = lax.axis_size(axis)
    return lax.ppermute(value, axis, [(i, (i + steps) % count) for i in range(count)])


def swap(value, axis):
    return lax.ppermute(value, axis, [(0, 1), (1, 0)])


def part_ways(value):
    count = lax.axis_size("x")
    up = [(i, (i + 1) % count) for i in range(count)]
    down = [(count + i, count + (i - 1) % count) for i in range(count)]
    return lax.ppermute(value, ("core", "x"), up + down)


def lanes(x, width):
    return jnp.concatenate([x] * (width // DH), axis=1)


def scores_of(q, k):
    return lax.dot_general(q, k, (((1,), (1,)), ((), ())), preferred_element_type=jnp.float32) * SCALE


def with_ones(v):
    return jnp.concatenate([v, jnp.ones(v.shape, v.dtype)], axis=1)


def absorb(h, s, v, m_ref, acc_ref):
    m_old = m_ref[h]
    m_new = jnp.maximum(m_old, jnp.max(s, axis=1, keepdims=True))
    p = jnp.exp2(s - lanes(m_new, s.shape[1])).astype(jnp.bfloat16)
    pv = jnp.dot(p, with_ones(v), preferred_element_type=jnp.float32)
    acc_ref[h] = acc_ref[h] * lanes(jnp.exp2(m_old - m_new), 2 * DH) + pv
    m_ref[h] = m_new


def reset(m_ref, acc_ref):
    m_ref[...] = jnp.full(m_ref.shape, NEG, jnp.float32)
    acc_ref[...] = jnp.zeros(acc_ref.shape, jnp.float32)


def log2_count(count):
    return jnp.where(count >= 4, 2.0, jnp.where(count >= 3, math.log2(3), jnp.where(count >= 2, 1.0, 0.0)))


def of_head(h):
    return slice(h * DH, (h + 1) * DH)


def absorb_memories(memories, lengths, counts, queries, m_ref, acc_ref):
    for (keys, values), length, count in zip(memories, lengths, counts):
        live, weight = jnp.where(count > 0, length, 0), log2_count(count)

        def fold(chunk, carry, keys=keys, values=values, live=live, weight=weight):
            start = pl.multiple_of(chunk * KEY_CHUNK, KEY_CHUNK)
            row = lax.broadcasted_iota(jnp.int32, (1, KEY_CHUNK), 1) + start
            bias = jnp.where(row < live, weight, NEG)
            for h in range(m_ref.shape[0]):
                k, v = (a[pl.ds(start, KEY_CHUNK), of_head(h)] for a in (keys, values))
                absorb(h, scores_of(queries(h), k) + bias, v, m_ref, acc_ref)
            return carry

        lax.fori_loop(0, (live + KEY_CHUNK - 1) // KEY_CHUNK, fold, 0)


def finish(out_ref, level_ref, m_ref, acc_ref):
    heads, rows = m_ref.shape[:2]
    level_ref[...] = jnp.zeros(level_ref.shape, jnp.float32)
    for h in range(heads):
        total = acc_ref[h, :, DH:]
        seen = total > 0
        safe = jnp.where(seen, total, 1.0)
        out_ref[:rows, of_head(h)] = (acc_ref[h, :, :DH] / safe).astype(jnp.bfloat16)
        rest = jnp.where(seen, m_ref[h] + jnp.log2(safe), NEG).T[:1, :]
        for i in range(3):
            term = rest.astype(jnp.bfloat16).astype(jnp.float32)
            level_ref[3 * h + i : 3 * h + i + 1, :rows] = term
            rest = rest - term
    out_ref[rows:, :] = level_ref[...].astype(jnp.bfloat16)


def home_kernel(offsets, lengths, q_ref, lk_ref, lv_ref, k0, v0, k1, v1, out_ref, m_ref, acc_ref, level_ref, *, half):
    core, document = lax.axis_index("core"), lax.axis_index(DOC)
    heads, rows = m_ref.shape[:2]
    first, keys = half * rows, (half + 1) * rows
    count = sum(jnp.where((offsets[0, i] == 1) & (core == 1), 1, 0) for i in range(offsets.shape[1]))
    reset(m_ref, acc_ref)

    def queries(h):
        return q_ref[first : first + rows, of_head(h)]

    seen = lax.broadcasted_iota(jnp.int32, (rows, keys), 0) + first >= lax.broadcasted_iota(jnp.int32, (rows, keys), 1)
    for h in range(heads):
        s = jnp.where(seen, scores_of(queries(h), lk_ref[:keys, of_head(h)]), NEG)
        absorb(h, s, lv_ref[:keys, of_head(h)], m_ref, acc_ref)
    live = lengths[document], lengths[document + 1 - 2 * core]
    absorb_memories(((k0, v0), (k1, v1)), live, (jnp.int32(1), count), queries, m_ref, acc_ref)
    finish(out_ref, level_ref, m_ref, acc_ref)


def guest_kernel(offsets, lengths, q_ref, k0, v0, k1, v1, *refs, back):
    *extra, m_ref, acc_ref, level_ref = refs
    core, document = lax.axis_index("core"), lax.axis_index(DOC)
    reset(m_ref, acc_ref)
    counts = [
        sum(jnp.where(offsets[0, i] == wanted, 1, 0) for i in range(offsets.shape[1]))
        for wanted in (back, back - 1 + 2 * core)
    ]
    live = lengths[document], lengths[document + 1 - 2 * core]
    absorb_memories(((k0, v0), (k1, v1)), live, counts, lambda h: q_ref[:, of_head(h)], m_ref, acc_ref)
    if len(extra) == 3:
        weights, out_ref, half_ref = extra
        half = half_ref.shape[0]
        half_ref[...] = weights[pl.ds(pl.multiple_of(core * half, half), half), :]
    else:
        (out_ref,) = extra
    finish(out_ref, level_ref, m_ref, acc_ref)


def on_chip(value):
    return pltpu.with_memory_space_constraint(value, pltpu.VMEM)


def kernel_call(kernel, scalars, arrays, outs, scratch):
    space = pl.BlockSpec(memory_space=pltpu.VMEM)
    return pl.pallas_call(
        kernel,
        grid_spec=pltpu.PrefetchScalarGridSpec(
            num_scalar_prefetch=len(scalars),
            grid=(),
            in_specs=[space] * len(arrays),
            out_specs=[space] * len(outs),
            scratch_shapes=scratch,
        ),
        out_shape=[pltpu.VMEM(shape, jnp.bfloat16) for shape in outs],
        compiler_params=pltpu.CompilerParams(vmem_limit_bytes=VMEM_LIMIT),
    )(*scalars, *arrays)


def attention(kernel, scalars, arrays, rows, width, extra=()):
    heads = width // DH
    scratch = [
        pltpu.VMEM((heads, rows, DH), jnp.float32),
        pltpu.VMEM((heads, rows, 2 * DH), jnp.float32),
        pltpu.VMEM((TAIL, width), jnp.float32),
    ]
    return kernel_call(kernel, scalars, arrays, [(rows + TAIL, width), *extra], scratch)


def merge_kernel(*refs):
    *homes, far_ref, near_ref = refs[:4]
    *tiles, share_ref, whole_ref = refs[4:]
    rows, width = whole_ref.shape
    heads, count = width // DH, len(tiles)
    half = rows // 2
    for n, home_ref in enumerate(homes):
        span = slice(n * half, (n + 1) * half)
        parts = [(home_ref, slice(0, half)), (far_ref, span), (near_ref, span)]
        tails = [part[-TAIL:, where].astype(jnp.float32) for part, where in parts]
        for h in range(heads):
            levels = [tail[3 * h : 3 * h + 1] + tail[3 * h + 1 : 3 * h + 2] + tail[3 * h + 2 : 3 * h + 3] for tail in tails]
            top = jnp.maximum(jnp.maximum(levels[0], levels[1]), levels[2])
            shares = [jnp.exp2(level - top) for level in levels]
            total = shares[0] + shares[1] + shares[2]
            for i, share in enumerate(shares):
                share_ref[n, 3 * h + i : 3 * h + i + 1, :] = share / total
        columns = share_ref[n].T
        for h in range(heads):
            mixed = 0.0
            for i, (part, where) in enumerate(parts):
                mixed = mixed + columns[:, 3 * h + i : 3 * h + i + 1] * part[where, of_head(h)].astype(jnp.float32)
            whole_ref[span, of_head(h)] = mixed.astype(whole_ref.dtype)
    block = half // count
    x, yh = lax.axis_index("x"), lax.axis_index("yh")
    for k, tile in enumerate(tiles):
        for n, side in enumerate((1 - yh, yh)):
            first = side * half + (x + k) % count * block
            tile[n * block : (n + 1) * block, :] = whole_ref[pl.ds(pl.multiple_of(first, block), block), :]


def merge(home0, home1, far, near):
    rows, width = far.shape[0] - TAIL, far.shape[1]
    count = lax.axis_size("x")
    scratch = [pltpu.VMEM((2, DH, rows // 2), jnp.float32), pltpu.VMEM((rows, width), jnp.bfloat16)]
    return kernel_call(merge_kernel, (), (home0, home1, far, near), [(rows // count, width)] * count, scratch)


def project_kernel(*refs, part):
    mine, below, opposite, above, own, near, near_other, far, far_other, *extra, out_ref = refs
    rows, half = out_ref.shape[0], far.shape[0]
    core = lax.axis_index("core")

    def tile(ref):
        return ref[part * rows : (part + 1) * rows, :]

    pairs = [
        (tile(mine), own),
        (jnp.where(core == 0, tile(below), tile(above)), near),
        (jnp.where(core == 0, tile(above), tile(below)), near_other),
        (jnp.where(core == 0, tile(opposite)[:, :half], tile(opposite)[:, half:]), far),
        (jnp.where(core == 0, tile(opposite)[:, half:], tile(opposite)[:, :half]), far_other),
    ]
    acc = sum(jnp.dot(a, w[...], preferred_element_type=jnp.float32) for a, w in pairs)
    for ref in extra:
        acc = acc + ref[...].astype(jnp.float32)
    out_ref[...] = acc.astype(out_ref.dtype)


def project(tiles, weights, extra, part):
    def kernel(*refs):
        project_kernel(*refs, part=part)

    out = (tiles[0].shape[0] // 2, weights[0].shape[1])
    return kernel_call(kernel, (), (*tiles, *weights, *extra), [out], [])[0]


def after(value, *others):
    return lax.optimization_barrier((value, *others))[0]


def step(queries, local_keys, local_values, mem_keys, mem_values, offsets, mem_lengths, out_weight):
    rows, width = queries.shape

    def moved(move, value, *where):
        value = move(value, *where)
        return on_chip(value) if value.dtype == jnp.bfloat16 else value

    query_far = moved(shift, queries, DOC, -4)
    query_near = moved(shift, queries, DOC, -2)
    offsets_far = moved(shift, offsets, DOC, -4)
    offsets_near = moved(shift, offsets, DOC, -2)
    other_keys = moved(swap, mem_keys, "core")
    other_values = moved(swap, mem_values, "core")
    memory = (on_chip(mem_keys), on_chip(mem_values), other_keys, other_values)
    local = (on_chip(queries), on_chip(local_keys), on_chip(local_values))
    near_weight = moved(part_ways, out_weight)

    def at_home(local, half):
        def kernel(*refs):
            home_kernel(*refs, half=half)

        return attention(kernel, (offsets, mem_lengths), (*local, *memory), rows // 2, width)[0]

    def guest(load, table, back, *weights):
        def kernel(*refs):
            guest_kernel(*refs, back=back)

        extra = [(w.shape[0] // 2, w.shape[1]) for w in weights]
        out, *rest = attention(kernel, (table, mem_lengths), (load, *memory, *weights), rows, width, extra)
        return moved(shift, out, DOC, back), out, *rest

    home0 = at_home(local, 0)
    from_far, far, *_ = guest(after(query_far, home0), offsets_far, 4)
    from_near, near, passed_on = guest(after(query_near, far), offsets_near, 2, near_weight)
    home1 = at_home((after(local[0], near), *local[1:]), 1)

    far_weight = moved(part_ways, passed_on)
    weights = [
        on_chip(out_weight),
        near_weight,
        moved(swap, after(near_weight, near), "core"),
        far_weight,
        moved(swap, far_weight, "core"),
    ]

    mine, *tiles = merge(home0, home1, from_far, from_near)
    tiles = mine, *(moved(shift, tile, "x", k) for k, tile in enumerate(tiles, 1))
    given = project(tiles, weights, (), 0)
    taken = swap(given, "yh")
    kept = project(tiles, weights, (), 1)
    return (kept.astype(jnp.float32) + taken.astype(jnp.float32)).astype(jnp.bfloat16)


def solution(mesh):
    split = Mesh(mesh.devices.reshape(-1, 2, 2, 2, 4), (*DOC, *HEAD))
    placed = (
        P(DOC, HEAD),
        P(DOC, HEAD),
        P(DOC, HEAD),
        P(DOC, HEAD),
        P(DOC, HEAD),
        P(DOC, None),
        P(),
        P(HEAD, None),
    )
    return jax.shard_map(step, mesh=split, in_specs=placed, out_specs=P((*DOC, *HEAD), None), check_vma=False)
```

```python
import math

import jax
import jax.numpy as jnp
from jax import lax
from jax.experimental import pallas as pl
from jax.experimental.pallas import tpu as pltpu
from jax.sharding import Mesh
from jax.sharding import PartitionSpec as P

DH = 128
DOC = ("z", "yl", "core")
HEAD = ("yh", "x")
NEG = -1e30
KEY_CHUNK = 512
TAIL = 16
SCALE = math.log2(math.e) / math.sqrt(DH)

VMEM_LIMIT = 24 * 2**20


def shift(value, axis, steps):
    count = lax.axis_size(axis)
    return lax.ppermute(value, axis, [(i, (i + steps) % count) for i in range(count)])


def swap(value, axis):
    return lax.ppermute(value, axis, [(0, 1), (1, 0)])


def part_ways(value):
    count = lax.axis_size("x")
    up = [(i, (i + 1) % count) for i in range(count)]
    down = [(count + i, count + (i - 1) % count) for i in range(count)]
    return lax.ppermute(value, ("core", "x"), up + down)


def lanes(x, width):
    return jnp.concatenate([x] * (width // DH), axis=1)


def scores_of(q, k):
    return lax.dot_general(q, k, (((1,), (1,)), ((), ())), preferred_element_type=jnp.float32) * SCALE


def with_ones(v):
    return jnp.concatenate([v, jnp.ones(v.shape, v.dtype)], axis=1)


def absorb(h, s, v, m_ref, acc_ref):
    m_old = m_ref[h]
    m_new = jnp.maximum(m_old, jnp.max(s, axis=1, keepdims=True))
    p = jnp.exp2(s - lanes(m_new, s.shape[1])).astype(jnp.bfloat16)
    pv = jnp.dot(p, with_ones(v), preferred_element_type=jnp.float32)
    acc_ref[h] = acc_ref[h] * lanes(jnp.exp2(m_old - m_new), 2 * DH) + pv
    m_ref[h] = m_new


def reset(m_ref, acc_ref):
    m_ref[...] = jnp.full(m_ref.shape, NEG, jnp.float32)
    acc_ref[...] = jnp.zeros(acc_ref.shape, jnp.float32)


def log2_count(count):
    return jnp.where(count >= 4, 2.0, jnp.where(count >= 3, math.log2(3), jnp.where(count >= 2, 1.0, 0.0)))


def of_head(h):
    return slice(h * DH, (h + 1) * DH)


def absorb_memories(memories, lengths, counts, queries, m_ref, acc_ref):
    for (keys, values), length, count in zip(memories, lengths, counts):
        live, weight = jnp.where(count > 0, length, 0), log2_count(count)

        def fold(chunk, carry, keys=keys, values=values, live=live, weight=weight):
            start = pl.multiple_of(chunk * KEY_CHUNK, KEY_CHUNK)
            row = lax.broadcasted_iota(jnp.int32, (1, KEY_CHUNK), 1) + start
            bias = jnp.where(row < live, weight, NEG)
            for h in range(m_ref.shape[0]):
                k, v = (a[pl.ds(start, KEY_CHUNK), of_head(h)] for a in (keys, values))
                absorb(h, scores_of(queries(h), k) + bias, v, m_ref, acc_ref)
            return carry

        lax.fori_loop(0, (live + KEY_CHUNK - 1) // KEY_CHUNK, fold, 0)


def finish(out_ref, level_ref, m_ref, acc_ref):
    heads, rows = m_ref.shape[:2]
    level_ref[...] = jnp.zeros(level_ref.shape, jnp.float32)
    for h in range(heads):
        total = acc_ref[h, :, DH:]
        seen = total > 0
        safe = jnp.where(seen, total, 1.0)
        out_ref[:rows, of_head(h)] = (acc_ref[h, :, :DH] / safe).astype(jnp.bfloat16)
        rest = jnp.where(seen, m_ref[h] + jnp.log2(safe), NEG).T[:1, :]
        for i in range(3):
            term = rest.astype(jnp.bfloat16).astype(jnp.float32)
            level_ref[3 * h + i : 3 * h + i + 1, :rows] = term
            rest = rest - term
    out_ref[rows:, :] = level_ref[...].astype(jnp.bfloat16)


def home_kernel(offsets, lengths, q_ref, lk_ref, lv_ref, k0, v0, k1, v1, out_ref, m_ref, acc_ref, level_ref, *, half):
    core, document = lax.axis_index("core"), lax.axis_index(DOC)
    heads, rows = m_ref.shape[:2]
    first, keys = half * rows, (half + 1) * rows
    count = sum(jnp.where((offsets[0, i] == 1) & (core == 1), 1, 0) for i in range(offsets.shape[1]))
    reset(m_ref, acc_ref)

    def queries(h):
        return q_ref[first : first + rows, of_head(h)]

    seen = lax.broadcasted_iota(jnp.int32, (rows, keys), 0) + first >= lax.broadcasted_iota(jnp.int32, (rows, keys), 1)
    for h in range(heads):
        s = jnp.where(seen, scores_of(queries(h), lk_ref[:keys, of_head(h)]), NEG)
        absorb(h, s, lv_ref[:keys, of_head(h)], m_ref, acc_ref)
    live = lengths[document], lengths[document + 1 - 2 * core]
    absorb_memories(((k0, v0), (k1, v1)), live, (jnp.int32(1), count), queries, m_ref, acc_ref)
    finish(out_ref, level_ref, m_ref, acc_ref)


def guest_kernel(offsets, lengths, q_ref, k0, v0, k1, v1, *refs, back):
    out_ref, m_ref, acc_ref, level_ref = refs
    core, document = lax.axis_index("core"), lax.axis_index(DOC)
    reset(m_ref, acc_ref)
    counts = [
        sum(jnp.where(offsets[0, i] == wanted, 1, 0) for i in range(offsets.shape[1]))
        for wanted in (back, back - 1 + 2 * core)
    ]
    live = lengths[document], lengths[document + 1 - 2 * core]
    absorb_memories(((k0, v0), (k1, v1)), live, counts, lambda h: q_ref[:, of_head(h)], m_ref, acc_ref)
    finish(out_ref, level_ref, m_ref, acc_ref)


def on_chip(value):
    return pltpu.with_memory_space_constraint(value, pltpu.VMEM)


def kernel_call(kernel, scalars, arrays, outs, scratch):
    space = pl.BlockSpec(memory_space=pltpu.VMEM)
    return pl.pallas_call(
        kernel,
        grid_spec=pltpu.PrefetchScalarGridSpec(
            num_scalar_prefetch=len(scalars),
            grid=(),
            in_specs=[space] * len(arrays),
            out_specs=[space] * len(outs),
            scratch_shapes=scratch,
        ),
        out_shape=[pltpu.VMEM(shape, jnp.bfloat16) for shape in outs],
        compiler_params=pltpu.CompilerParams(vmem_limit_bytes=VMEM_LIMIT),
    )(*scalars, *arrays)


def attention(kernel, scalars, arrays, rows, width):
    heads = width // DH
    scratch = [
        pltpu.VMEM((heads, rows, DH), jnp.float32),
        pltpu.VMEM((heads, rows, 2 * DH), jnp.float32),
        pltpu.VMEM((TAIL, width), jnp.float32),
    ]
    return kernel_call(kernel, scalars, arrays, [(rows + TAIL, width)], scratch)[0]


def load_kernel(*refs):
    *pairs, sems = refs
    count = len(pairs) // 2
    copies = [pltpu.make_async_copy(pairs[i], pairs[count + i], sems.at[i]) for i in range(count)]
    for copy in copies:
        copy.start()
    for copy in copies:
        copy.wait()


def load(*arrays):
    return pl.pallas_call(
        load_kernel,
        in_specs=[pl.BlockSpec(memory_space=pltpu.HBM)] * len(arrays),
        out_specs=[pl.BlockSpec(memory_space=pltpu.VMEM)] * len(arrays),
        out_shape=[pltpu.VMEM(a.shape, a.dtype) for a in arrays],
        scratch_shapes=[pltpu.SemaphoreType.DMA((len(arrays),))],
        compiler_params=pltpu.CompilerParams(vmem_limit_bytes=VMEM_LIMIT),
        name="load",
    )(*(pltpu.with_memory_space_constraint(a, pltpu.HBM) for a in arrays))


def pass_on_kernel(weights, half_ref):
    half = half_ref.shape[0]
    half_ref[...] = weights[pl.ds(pl.multiple_of(lax.axis_index("core") * half, half), half), :]


def pass_on(weights):
    depth, width = weights.shape
    return kernel_call(pass_on_kernel, (), (weights,), [(depth // 2, width)], [])[0]


def merge_kernel(*refs):
    *homes, far_ref, near_ref = refs[:4]
    *tiles, share_ref, whole_ref = refs[4:]
    rows, width = whole_ref.shape
    heads, count = width // DH, len(tiles)
    half = rows // 2
    for n, home_ref in enumerate(homes):
        span = slice(n * half, (n + 1) * half)
        parts = [(home_ref, slice(0, half)), (far_ref, span), (near_ref, span)]
        tails = [part[-TAIL:, where].astype(jnp.float32) for part, where in parts]
        for h in range(heads):
            levels = [tail[3 * h : 3 * h + 1] + tail[3 * h + 1 : 3 * h + 2] + tail[3 * h + 2 : 3 * h + 3] for tail in tails]
            top = jnp.maximum(jnp.maximum(levels[0], levels[1]), levels[2])
            shares = [jnp.exp2(level - top) for level in levels]
            total = shares[0] + shares[1] + shares[2]
            for i, share in enumerate(shares):
                share_ref[n, 3 * h + i : 3 * h + i + 1, :] = share / total
        columns = share_ref[n].T
        for h in range(heads):
            mixed = 0.0
            for i, (part, where) in enumerate(parts):
                mixed = mixed + columns[:, 3 * h + i : 3 * h + i + 1] * part[where, of_head(h)].astype(jnp.float32)
            whole_ref[span, of_head(h)] = mixed.astype(whole_ref.dtype)
    block = half // count
    x, yh = lax.axis_index("x"), lax.axis_index("yh")
    for k, tile in enumerate(tiles):
        for n, side in enumerate((1 - yh, yh)):
            first = side * half + (x + k) % count * block
            tile[n * block : (n + 1) * block, :] = whole_ref[pl.ds(pl.multiple_of(first, block), block), :]


def merge(home0, home1, far, near):
    rows, width = far.shape[0] - TAIL, far.shape[1]
    count = lax.axis_size("x")
    scratch = [pltpu.VMEM((2, DH, rows // 2), jnp.float32), pltpu.VMEM((rows, width), jnp.bfloat16)]
    return kernel_call(merge_kernel, (), (home0, home1, far, near), [(rows // count, width)] * count, scratch)


def project_kernel(*refs, part):
    mine, below, opposite, above, own, near, near_other, far, far_other, *extra, out_ref = refs
    rows, half = out_ref.shape[0], far.shape[0]
    core = lax.axis_index("core")

    def tile(ref):
        return ref[part * rows : (part + 1) * rows, :]

    pairs = [
        (tile(mine), own),
        (jnp.where(core == 0, tile(below), tile(above)), near),
        (jnp.where(core == 0, tile(above), tile(below)), near_other),
        (jnp.where(core == 0, tile(opposite)[:, :half], tile(opposite)[:, half:]), far),
        (jnp.where(core == 0, tile(opposite)[:, half:], tile(opposite)[:, :half]), far_other),
    ]
    acc = sum(jnp.dot(a, w[...], preferred_element_type=jnp.float32) for a, w in pairs)
    for ref in extra:
        acc = acc + ref[...].astype(jnp.float32)
    out_ref[...] = acc.astype(out_ref.dtype)


def project(tiles, weights, extra, part):
    def kernel(*refs):
        project_kernel(*refs, part=part)

    out = (tiles[0].shape[0] // 2, weights[0].shape[1])
    return kernel_call(kernel, (), (*tiles, *weights, *extra), [out], [])[0]


def after(value, *others):
    return lax.optimization_barrier((value, *others))[0]


def step(queries, local_keys, local_values, mem_keys, mem_values, offsets, mem_lengths, out_weight):
    rows, width = queries.shape

    def moved(move, value, *where):
        value = move(value, *where)
        return on_chip(value) if value.dtype == jnp.bfloat16 else value

    query_far = moved(shift, queries, DOC, -4)
    query_near = moved(shift, queries, DOC, -2)
    offsets_far = moved(shift, offsets, DOC, -4)
    offsets_near = moved(shift, offsets, DOC, -2)
    other_keys = moved(swap, mem_keys, "core")
    other_values = moved(swap, mem_values, "core")
    near_weight = moved(part_ways, out_weight)
    own_keys, own_values, own_weight, *local = load(mem_keys, mem_values, out_weight, queries, local_keys, local_values)
    memory = (own_keys, own_values, other_keys, other_values)

    def at_home(local, half):
        def kernel(*refs):
            home_kernel(*refs, half=half)

        return attention(kernel, (offsets, mem_lengths), (*local, *memory), rows // 2, width)

    def guest(load, table, back):
        def kernel(*refs):
            guest_kernel(*refs, back=back)

        out = attention(kernel, (table, mem_lengths), (load, *memory), rows, width)
        return moved(shift, out, DOC, back), out

    home0 = at_home(local, 0)
    from_far, far = guest(after(query_far, home0), offsets_far, 4)
    from_near, near = guest(after(query_near, far), offsets_near, 2)

    near_weight = after(near_weight, near)
    passed_on = pass_on(near_weight)
    home1 = at_home((after(local[0], near, passed_on), *local[1:]), 1)
    far_weight = moved(part_ways, passed_on)
    weights = [own_weight, near_weight, moved(swap, near_weight, "core"), far_weight, moved(swap, far_weight, "core")]

    mine, *tiles = merge(home0, home1, from_far, from_near)
    tiles = mine, *(moved(shift, tile, "x", k) for k, tile in enumerate(tiles, 1))
    given = project(tiles, weights, (), 0)
    taken = swap(given, "yh")
    kept = project(tiles, weights, (), 1)
    return (kept.astype(jnp.float32) + taken.astype(jnp.float32)).astype(jnp.bfloat16)


def solution(mesh):
    split = Mesh(mesh.devices.reshape(-1, 2, 2, 2, 4), (*DOC, *HEAD))
    placed = (
        P(DOC, HEAD),
        P(DOC, HEAD),
        P(DOC, HEAD),
        P(DOC, HEAD),
        P(DOC, HEAD),
        P(DOC, None),
        P(),
        P(HEAD, None),
    )
    return jax.shard_map(step, mesh=split, in_specs=placed, out_specs=P((*DOC, *HEAD), None), check_vma=False)
```

```python
import math

import jax
import jax.numpy as jnp
from jax import lax
from jax.experimental import pallas as pl
from jax.experimental.pallas import tpu as pltpu
from jax.sharding import Mesh
from jax.sharding import PartitionSpec as P

DH = 128
DOC = ("z", "yl", "core")
HEAD = ("yh", "x")
NEG = -1e30
KEY_CHUNK = 512
TAIL = 16
SCALE = math.log2(math.e) / math.sqrt(DH)

VMEM_LIMIT = 24 * 2**20


def shift(value, axis, steps):
    count = lax.axis_size(axis)
    return lax.ppermute(value, axis, [(i, (i + steps) % count) for i in range(count)])


def swap(value, axis):
    return lax.ppermute(value, axis, [(0, 1), (1, 0)])


def part_ways(value):
    count = lax.axis_size("x")
    up = [(i, (i + 1) % count) for i in range(count)]
    down = [(count + i, count + (i - 1) % count) for i in range(count)]
    return lax.ppermute(value, ("core", "x"), up + down)


def lanes(x, width):
    return jnp.concatenate([x] * (width // DH), axis=1)


def scores_of(q, k):
    return lax.dot_general(q, k, (((1,), (1,)), ((), ())), preferred_element_type=jnp.float32) * SCALE


def with_ones(v):
    return jnp.concatenate([v, jnp.ones(v.shape, v.dtype)], axis=1)


def absorb(h, s, v, m_ref, acc_ref):
    m_old = m_ref[h]
    m_new = jnp.maximum(m_old, jnp.max(s, axis=1, keepdims=True))
    p = jnp.exp2(s - lanes(m_new, s.shape[1])).astype(jnp.bfloat16)
    pv = jnp.dot(p, with_ones(v), preferred_element_type=jnp.float32)
    acc_ref[h] = acc_ref[h] * lanes(jnp.exp2(m_old - m_new), 2 * DH) + pv
    m_ref[h] = m_new


def reset(m_ref, acc_ref):
    m_ref[...] = jnp.full(m_ref.shape, NEG, jnp.float32)
    acc_ref[...] = jnp.zeros(acc_ref.shape, jnp.float32)


def log2_count(count):
    return jnp.where(count >= 4, 2.0, jnp.where(count >= 3, math.log2(3), jnp.where(count >= 2, 1.0, 0.0)))


def of_head(h):
    return slice(h * DH, (h + 1) * DH)


def absorb_memories(memories, lengths, counts, queries, m_ref, acc_ref):
    for (keys, values), length, count in zip(memories, lengths, counts):
        live, weight = jnp.where(count > 0, length, 0), log2_count(count)

        def fold(chunk, carry, keys=keys, values=values, live=live, weight=weight):
            start = pl.multiple_of(chunk * KEY_CHUNK, KEY_CHUNK)
            row = lax.broadcasted_iota(jnp.int32, (1, KEY_CHUNK), 1) + start
            bias = jnp.where(row < live, weight, NEG)
            for h in range(m_ref.shape[0]):
                k, v = (a[pl.ds(start, KEY_CHUNK), of_head(h)] for a in (keys, values))
                absorb(h, scores_of(queries(h), k) + bias, v, m_ref, acc_ref)
            return carry

        lax.fori_loop(0, (live + KEY_CHUNK - 1) // KEY_CHUNK, fold, 0)


def finish(out_refs, level_ref, m_ref, acc_ref):
    heads = m_ref.shape[0]
    for n, out_ref in enumerate(out_refs):
        rows = out_ref.shape[0] - TAIL
        span = slice(n * rows, (n + 1) * rows)
        level_ref[...] = jnp.zeros(level_ref.shape, jnp.float32)
        for h in range(heads):
            total = acc_ref[h, span, DH:]
            seen = total > 0
            safe = jnp.where(seen, total, 1.0)
            out_ref[:rows, of_head(h)] = (acc_ref[h, span, :DH] / safe).astype(jnp.bfloat16)
            rest = jnp.where(seen, m_ref[h, span, :] + jnp.log2(safe), NEG).T[:1, :]
            for i in range(3):
                term = rest.astype(jnp.bfloat16).astype(jnp.float32)
                level_ref[3 * h + i : 3 * h + i + 1, :rows] = term
                rest = rest - term
        out_ref[rows:, :] = level_ref[...].astype(jnp.bfloat16)


def halves(ref, h):
    rows, yh = ref.shape[0] // 2, lax.axis_index("yh")
    return [ref[pl.ds(pl.multiple_of(half * rows, rows), rows), of_head(h)] for half in (1 - yh, yh)]


def home_kernel(offsets, lengths, q_ref, lk_ref, lv_ref, k0, v0, k1, v1, *refs, half):
    *out_refs, m_ref, acc_ref, level_ref = refs
    core, document = lax.axis_index("core"), lax.axis_index(DOC)
    heads, rows = m_ref.shape[:2]
    keys, yh = lk_ref.shape[0], lax.axis_index("yh")
    first = (yh if half else 1 - yh) * rows
    count = sum(jnp.where((offsets[0, i] == 1) & (core == 1), 1, 0) for i in range(offsets.shape[1]))
    reset(m_ref, acc_ref)

    def queries(h):
        return halves(q_ref, h)[half]

    seen = lax.broadcasted_iota(jnp.int32, (rows, keys), 0) + first >= lax.broadcasted_iota(jnp.int32, (rows, keys), 1)
    for h in range(heads):
        s = jnp.where(seen, scores_of(queries(h), lk_ref[:, of_head(h)]), NEG)
        absorb(h, s, lv_ref[:, of_head(h)], m_ref, acc_ref)
    live = lengths[document], lengths[document + 1 - 2 * core]
    absorb_memories(((k0, v0), (k1, v1)), live, (jnp.int32(1), count), queries, m_ref, acc_ref)
    finish(out_refs, level_ref, m_ref, acc_ref)


def guest_kernel(offsets, lengths, q_ref, k0, v0, k1, v1, *refs, back):
    *out_refs, m_ref, acc_ref, level_ref = refs
    core, document = lax.axis_index("core"), lax.axis_index(DOC)
    reset(m_ref, acc_ref)
    counts = [
        sum(jnp.where(offsets[0, i] == wanted, 1, 0) for i in range(offsets.shape[1]))
        for wanted in (back, back - 1 + 2 * core)
    ]
    live = lengths[document], lengths[document + 1 - 2 * core]
    absorb_memories(((k0, v0), (k1, v1)), live, counts, lambda h: jnp.concatenate(halves(q_ref, h), axis=0), m_ref, acc_ref)
    finish(out_refs, level_ref, m_ref, acc_ref)


def on_chip(value):
    return pltpu.with_memory_space_constraint(value, pltpu.VMEM)


def kernel_call(kernel, scalars, arrays, outs, scratch):
    space = pl.BlockSpec(memory_space=pltpu.VMEM)
    return pl.pallas_call(
        kernel,
        grid_spec=pltpu.PrefetchScalarGridSpec(
            num_scalar_prefetch=len(scalars),
            grid=(),
            in_specs=[space] * len(arrays),
            out_specs=[space] * len(outs),
            scratch_shapes=scratch,
        ),
        out_shape=[pltpu.VMEM(shape, jnp.bfloat16) for shape in outs],
        compiler_params=pltpu.CompilerParams(vmem_limit_bytes=VMEM_LIMIT),
    )(*scalars, *arrays)


def attention(kernel, scalars, arrays, rows, width, parts=1):
    heads = width // DH
    scratch = [
        pltpu.VMEM((heads, rows, DH), jnp.float32),
        pltpu.VMEM((heads, rows, 2 * DH), jnp.float32),
        pltpu.VMEM((TAIL, width), jnp.float32),
    ]
    return kernel_call(kernel, scalars, arrays, [(rows // parts + TAIL, width)] * parts, scratch)


def load_kernel(*refs):
    *pairs, sems = refs
    count = len(pairs) // 2
    copies = [pltpu.make_async_copy(pairs[i], pairs[count + i], sems.at[i]) for i in range(count)]
    for copy in copies:
        copy.start()
    for copy in copies:
        copy.wait()


def load(*arrays):
    return pl.pallas_call(
        load_kernel,
        in_specs=[pl.BlockSpec(memory_space=pltpu.HBM)] * len(arrays),
        out_specs=[pl.BlockSpec(memory_space=pltpu.VMEM)] * len(arrays),
        out_shape=[pltpu.VMEM(a.shape, a.dtype) for a in arrays],
        scratch_shapes=[pltpu.SemaphoreType.DMA((len(arrays),))],
        compiler_params=pltpu.CompilerParams(vmem_limit_bytes=VMEM_LIMIT),
        name="load",
    )(*(pltpu.with_memory_space_constraint(a, pltpu.HBM) for a in arrays))


def pass_on_kernel(weights, half_ref):
    half = half_ref.shape[0]
    half_ref[...] = weights[pl.ds(pl.multiple_of(lax.axis_index("core") * half, half), half), :]


def pass_on(weights):
    depth, width = weights.shape
    return kernel_call(pass_on_kernel, (), (weights,), [(depth // 2, width)], [])[0]


def merge_kernel(home_ref, near_ref, far_ref, *refs, half):
    *tiles, share_ref, whole_ref = refs
    rows, width = whole_ref.shape
    heads, count = width // DH, len(tiles)
    first = slice(0, rows)
    parts = [(home_ref, first), (far_ref, slice(half * rows, (half + 1) * rows)), (near_ref, first)]
    tails = [part[-TAIL:, where].astype(jnp.float32) for part, where in parts]
    for h in range(heads):
        levels = [tail[3 * h : 3 * h + 1] + tail[3 * h + 1 : 3 * h + 2] + tail[3 * h + 2 : 3 * h + 3] for tail in tails]
        top = jnp.maximum(jnp.maximum(levels[0], levels[1]), levels[2])
        shares = [jnp.exp2(level - top) for level in levels]
        total = shares[0] + shares[1] + shares[2]
        for i, share in enumerate(shares):
            share_ref[3 * h + i : 3 * h + i + 1, :] = share / total
    columns = share_ref[...].T
    for h in range(heads):
        mixed = 0.0
        for i, (part, where) in enumerate(parts):
            mixed = mixed + columns[:, 3 * h + i : 3 * h + i + 1] * part[where, of_head(h)].astype(jnp.float32)
        whole_ref[:, of_head(h)] = mixed.astype(whole_ref.dtype)
    block, x = rows // count, lax.axis_index("x")
    for k, tile in enumerate(tiles):
        tile[...] = whole_ref[pl.ds(pl.multiple_of((x + k) % count * block, block), block), :]


def merge(home, near, far, half):
    def kernel(*refs):
        merge_kernel(*refs, half=half)

    rows, width = home.shape[0] - TAIL, home.shape[1]
    count = lax.axis_size("x")
    scratch = [pltpu.VMEM((DH, rows), jnp.float32), pltpu.VMEM((rows, width), jnp.bfloat16)]
    return kernel_call(kernel, (), (home, near, far), [(rows // count, width)] * count, scratch)


def project_kernel(*refs):
    mine, below, opposite, above, own, near, near_other, far, far_other, out_ref = refs
    half = far.shape[0]
    core = lax.axis_index("core")

    pairs = [
        (mine[...], own),
        (jnp.where(core == 0, below[...], above[...]), near),
        (jnp.where(core == 0, above[...], below[...]), near_other),
        (jnp.where(core == 0, opposite[:, :half], opposite[:, half:]), far),
        (jnp.where(core == 0, opposite[:, half:], opposite[:, :half]), far_other),
    ]
    acc = sum(jnp.dot(a, w[...], preferred_element_type=jnp.float32) for a, w in pairs)
    out_ref[...] = acc.astype(out_ref.dtype)


def project(tiles, weights):
    out = (tiles[0].shape[0], weights[0].shape[1])
    return kernel_call(project_kernel, (), (*tiles, *weights), [out], [])[0]


def after(value, *others):
    return lax.optimization_barrier((value, *others))[0]


def step(queries, local_keys, local_values, mem_keys, mem_values, offsets, mem_lengths, out_weight):
    rows, width = queries.shape

    def moved(move, value, *where):
        value = move(value, *where)
        return on_chip(value) if value.dtype == jnp.bfloat16 else value

    query_far = moved(shift, queries, DOC, -4)
    query_near = moved(shift, queries, DOC, -2)
    offsets_far = moved(shift, offsets, DOC, -4)
    offsets_near = moved(shift, offsets, DOC, -2)
    other_keys = moved(swap, mem_keys, "core")
    other_values = moved(swap, mem_values, "core")
    near_weight = moved(part_ways, out_weight)
    own_keys, own_values, own_weight, *local = load(mem_keys, mem_values, out_weight, queries, local_keys, local_values)
    memory = (own_keys, own_values, other_keys, other_values)

    def at_home(local, half):
        def kernel(*refs):
            home_kernel(*refs, half=half)

        return attention(kernel, (offsets, mem_lengths), (*local, *memory), rows // 2, width)[0]

    def guest(load, table, back, parts=1):
        def kernel(*refs):
            guest_kernel(*refs, back=back)

        return attention(kernel, (table, mem_lengths), (load, *memory), rows, width, parts)

    home0 = at_home(local, 0)
    (far,) = guest(after(query_far, home0), offsets_far, 4)
    from_far = moved(shift, far, DOC, 4)
    near = guest(after(query_near, far), offsets_near, 2, 2)
    from_near = [moved(shift, out, DOC, 2) for out in near]

    near_weight = after(near_weight, *near)
    passed_on = pass_on(near_weight)
    home1 = at_home((after(local[0], *near, passed_on), *local[1:]), 1)
    far_weight = moved(part_ways, passed_on)
    weights = [own_weight, near_weight, moved(swap, near_weight, "core"), far_weight, moved(swap, far_weight, "core")]

    def tiles_of(home, near, half):
        mine, *tiles = merge(home, near, from_far, half)
        return mine, *(moved(shift, tile, "x", k) for k, tile in enumerate(tiles, 1))

    given = tiles_of(after(home0, home1), from_near[0], 0)
    kept = tiles_of(home1, after(from_near[1], given[0]), 1)
    given = project(given, weights)
    taken = swap(given, "yh")
    kept = project(kept, weights)
    return (kept.astype(jnp.float32) + taken.astype(jnp.float32)).astype(jnp.bfloat16)


def solution(mesh):
    split = Mesh(mesh.devices.reshape(-1, 2, 2, 2, 4), (*DOC, *HEAD))
    placed = (
        P(DOC, HEAD),
        P(DOC, HEAD),
        P(DOC, HEAD),
        P(DOC, HEAD),
        P(DOC, HEAD),
        P(DOC, None),
        P(),
        P(HEAD, None),
    )
    return jax.shard_map(step, mesh=split, in_specs=placed, out_specs=P((*DOC, *HEAD), None), check_vma=False)
```

```python
import math

import jax
import jax.numpy as jnp
from jax import lax
from jax.experimental import pallas as pl
from jax.experimental.pallas import tpu as pltpu
from jax.sharding import Mesh
from jax.sharding import PartitionSpec as P

DH = 128
DOC = ("z", "yl", "core")
HEAD = ("yh", "x")
NEG = -1e30
KEY_CHUNK = 512
TAIL = 16
SCALE = math.log2(math.e) / math.sqrt(DH)

VMEM_LIMIT = 24 * 2**20


def shift(value, axis, steps):
    count = lax.axis_size(axis)
    return lax.ppermute(value, axis, [(i, (i + steps) % count) for i in range(count)])


def swap(value, axis):
    return lax.ppermute(value, axis, [(0, 1), (1, 0)])


def part_ways(value):
    count = lax.axis_size("x")
    up = [(i, (i + 1) % count) for i in range(count)]
    down = [(count + i, count + (i - 1) % count) for i in range(count)]
    return lax.ppermute(value, ("core", "x"), up + down)


def lanes(x, width):
    return jnp.concatenate([x] * (width // DH), axis=1)


def scores_of(q, k):
    return lax.dot_general(q, k, (((1,), (1,)), ((), ())), preferred_element_type=jnp.float32) * SCALE


def with_ones(v):
    return jnp.concatenate([v, jnp.ones(v.shape, v.dtype)], axis=1)


def absorb(h, s, v, m_ref, acc_ref):
    m_old = m_ref[h]
    m_new = jnp.maximum(m_old, jnp.max(s, axis=1, keepdims=True))
    p = jnp.exp2(s - lanes(m_new, s.shape[1])).astype(jnp.bfloat16)
    pv = jnp.dot(p, with_ones(v), preferred_element_type=jnp.float32)
    acc_ref[h] = acc_ref[h] * lanes(jnp.exp2(m_old - m_new), 2 * DH) + pv
    m_ref[h] = m_new


def reset(m_ref, acc_ref):
    m_ref[...] = jnp.full(m_ref.shape, NEG, jnp.float32)
    acc_ref[...] = jnp.zeros(acc_ref.shape, jnp.float32)


def log2_count(count):
    return jnp.where(count >= 4, 2.0, jnp.where(count >= 3, math.log2(3), jnp.where(count >= 2, 1.0, 0.0)))


def of_head(h):
    return slice(h * DH, (h + 1) * DH)


def absorb_memories(memories, lengths, counts, queries, m_ref, acc_ref):
    for (keys, values), length, count in zip(memories, lengths, counts):
        live, weight = jnp.where(count > 0, length, 0), log2_count(count)

        def fold(chunk, carry, keys=keys, values=values, live=live, weight=weight):
            start = pl.multiple_of(chunk * KEY_CHUNK, KEY_CHUNK)
            row = lax.broadcasted_iota(jnp.int32, (1, KEY_CHUNK), 1) + start
            bias = jnp.where(row < live, weight, NEG)
            for h in range(m_ref.shape[0]):
                k, v = (a[pl.ds(start, KEY_CHUNK), of_head(h)] for a in (keys, values))
                absorb(h, scores_of(queries(h), k) + bias, v, m_ref, acc_ref)
            return carry

        lax.fori_loop(0, (live + KEY_CHUNK - 1) // KEY_CHUNK, fold, 0)


def finish(out_ref, level_ref, m_ref, acc_ref):
    heads, rows = m_ref.shape[:2]
    level_ref[...] = jnp.zeros(level_ref.shape, jnp.float32)
    for h in range(heads):
        total = acc_ref[h, :, DH:]
        seen = total > 0
        safe = jnp.where(seen, total, 1.0)
        out_ref[:rows, of_head(h)] = (acc_ref[h, :, :DH] / safe).astype(jnp.bfloat16)
        rest = jnp.where(seen, m_ref[h] + jnp.log2(safe), NEG).T[:1, :]
        for i in range(3):
            term = rest.astype(jnp.bfloat16).astype(jnp.float32)
            level_ref[3 * h + i : 3 * h + i + 1, :rows] = term
            rest = rest - term
    out_ref[rows:, :] = level_ref[...].astype(jnp.bfloat16)


def home_kernel(offsets, lengths, q_ref, lk_ref, lv_ref, k0, v0, k1, v1, out_ref, m_ref, acc_ref, level_ref, *, half):
    core, document = lax.axis_index("core"), lax.axis_index(DOC)
    heads, rows = m_ref.shape[:2]
    first, keys = half * rows, (half + 1) * rows
    count = sum(jnp.where((offsets[0, i] == 1) & (core == 1), 1, 0) for i in range(offsets.shape[1]))
    reset(m_ref, acc_ref)

    def queries(h):
        return q_ref[first : first + rows, of_head(h)]

    seen = lax.broadcasted_iota(jnp.int32, (rows, keys), 0) + first >= lax.broadcasted_iota(jnp.int32, (rows, keys), 1)
    for h in range(heads):
        s = jnp.where(seen, scores_of(queries(h), lk_ref[:keys, of_head(h)]), NEG)
        absorb(h, s, lv_ref[:keys, of_head(h)], m_ref, acc_ref)
    live = lengths[document], lengths[document + 1 - 2 * core]
    absorb_memories(((k0, v0), (k1, v1)), live, (jnp.int32(1), count), queries, m_ref, acc_ref)
    finish(out_ref, level_ref, m_ref, acc_ref)


def guest_kernel(offsets, lengths, q_ref, k0, v0, k1, v1, *refs, back, first):
    out_ref, m_ref, acc_ref, level_ref = refs
    core, document = lax.axis_index("core"), lax.axis_index(DOC)
    span = slice(first, first + m_ref.shape[1])
    reset(m_ref, acc_ref)
    counts = [
        sum(jnp.where(offsets[0, i] == wanted, 1, 0) for i in range(offsets.shape[1]))
        for wanted in (back, back - 1 + 2 * core)
    ]
    live = lengths[document], lengths[document + 1 - 2 * core]
    absorb_memories(((k0, v0), (k1, v1)), live, counts, lambda h: q_ref[span, of_head(h)], m_ref, acc_ref)
    finish(out_ref, level_ref, m_ref, acc_ref)


def on_chip(value):
    return pltpu.with_memory_space_constraint(value, pltpu.VMEM)


def kernel_call(kernel, scalars, arrays, outs, scratch):
    space = pl.BlockSpec(memory_space=pltpu.VMEM)
    return pl.pallas_call(
        kernel,
        grid_spec=pltpu.PrefetchScalarGridSpec(
            num_scalar_prefetch=len(scalars),
            grid=(),
            in_specs=[space] * len(arrays),
            out_specs=[space] * len(outs),
            scratch_shapes=scratch,
        ),
        out_shape=[pltpu.VMEM(shape, jnp.bfloat16) for shape in outs],
        compiler_params=pltpu.CompilerParams(vmem_limit_bytes=VMEM_LIMIT),
    )(*scalars, *arrays)


def attention(kernel, scalars, arrays, rows, width):
    heads = width // DH
    scratch = [
        pltpu.VMEM((heads, rows, DH), jnp.float32),
        pltpu.VMEM((heads, rows, 2 * DH), jnp.float32),
        pltpu.VMEM((TAIL, width), jnp.float32),
    ]
    return kernel_call(kernel, scalars, arrays, [(rows + TAIL, width)], scratch)[0]


def load_kernel(*refs):
    *pairs, sems = refs
    count = len(pairs) // 2
    copies = [pltpu.make_async_copy(pairs[i], pairs[count + i], sems.at[i]) for i in range(count)]
    for copy in copies:
        copy.start()
    for copy in copies:
        copy.wait()


def load(*arrays):
    return pl.pallas_call(
        load_kernel,
        in_specs=[pl.BlockSpec(memory_space=pltpu.HBM)] * len(arrays),
        out_specs=[pl.BlockSpec(memory_space=pltpu.VMEM)] * len(arrays),
        out_shape=[pltpu.VMEM(a.shape, a.dtype) for a in arrays],
        scratch_shapes=[pltpu.SemaphoreType.DMA((len(arrays),))],
        compiler_params=pltpu.CompilerParams(vmem_limit_bytes=VMEM_LIMIT),
        name="load",
    )(*(pltpu.with_memory_space_constraint(a, pltpu.HBM) for a in arrays))


def pass_on_kernel(weights, half_ref):
    half = half_ref.shape[0]
    half_ref[...] = weights[pl.ds(pl.multiple_of(lax.axis_index("core") * half, half), half), :]


def pass_on(weights):
    depth, width = weights.shape
    return kernel_call(pass_on_kernel, (), (weights,), [(depth // 2, width)], [])[0]


def merge_kernel(home0, home1, near0, near1, far_ref, *refs):
    *tiles, share_ref, whole_ref = refs
    rows, width = whole_ref.shape
    heads, count = width // DH, len(tiles)
    half = rows // 2
    for n, (home_ref, near_ref) in enumerate(((home0, near0), (home1, near1))):
        first, span = slice(0, half), slice(n * half, (n + 1) * half)
        parts = [(home_ref, first), (far_ref, span), (near_ref, first)]
        tails = [part[-TAIL:, where].astype(jnp.float32) for part, where in parts]
        for h in range(heads):
            levels = [tail[3 * h : 3 * h + 1] + tail[3 * h + 1 : 3 * h + 2] + tail[3 * h + 2 : 3 * h + 3] for tail in tails]
            top = jnp.maximum(jnp.maximum(levels[0], levels[1]), levels[2])
            shares = [jnp.exp2(level - top) for level in levels]
            total = shares[0] + shares[1] + shares[2]
            for i, share in enumerate(shares):
                share_ref[n, 3 * h + i : 3 * h + i + 1, :] = share / total
        columns = share_ref[n].T
        for h in range(heads):
            mixed = 0.0
            for i, (part, where) in enumerate(parts):
                mixed = mixed + columns[:, 3 * h + i : 3 * h + i + 1] * part[where, of_head(h)].astype(jnp.float32)
            whole_ref[span, of_head(h)] = mixed.astype(whole_ref.dtype)
    block = half // count
    x, yh = lax.axis_index("x"), lax.axis_index("yh")
    for k, tile in enumerate(tiles):
        for n, side in enumerate((1 - yh, yh)):
            first = side * half + (x + k) % count * block
            tile[n * block : (n + 1) * block, :] = whole_ref[pl.ds(pl.multiple_of(first, block), block), :]


def merge(homes, nears, far):
    rows, width = far.shape[0] - TAIL, far.shape[1]
    count = lax.axis_size("x")
    scratch = [pltpu.VMEM((2, DH, rows // 2), jnp.float32), pltpu.VMEM((rows, width), jnp.bfloat16)]
    return kernel_call(merge_kernel, (), (*homes, *nears, far), [(rows // count, width)] * count, scratch)


def project_kernel(*refs, part):
    mine, below, opposite, above, own, near, near_other, far, far_other, *extra, out_ref = refs
    rows, half = out_ref.shape[0], far.shape[0]
    core = lax.axis_index("core")

    def tile(ref):
        return ref[part * rows : (part + 1) * rows, :]

    pairs = [
        (tile(mine), own),
        (jnp.where(core == 0, tile(below), tile(above)), near),
        (jnp.where(core == 0, tile(above), tile(below)), near_other),
        (jnp.where(core == 0, tile(opposite)[:, :half], tile(opposite)[:, half:]), far),
        (jnp.where(core == 0, tile(opposite)[:, half:], tile(opposite)[:, :half]), far_other),
    ]
    acc = sum(jnp.dot(a, w[...], preferred_element_type=jnp.float32) for a, w in pairs)
    for ref in extra:
        acc = acc + ref[...].astype(jnp.float32)
    out_ref[...] = acc.astype(out_ref.dtype)


def project(tiles, weights, extra, part):
    def kernel(*refs):
        project_kernel(*refs, part=part)

    out = (tiles[0].shape[0] // 2, weights[0].shape[1])
    return kernel_call(kernel, (), (*tiles, *weights, *extra), [out], [])[0]


def after(value, *others):
    return lax.optimization_barrier((value, *others))[0]


def step(queries, local_keys, local_values, mem_keys, mem_values, offsets, mem_lengths, out_weight):
    rows, width = queries.shape

    def moved(move, value, *where):
        value = move(value, *where)
        return on_chip(value) if value.dtype == jnp.bfloat16 else value

    query_far = moved(shift, queries, DOC, -4)
    query_near = moved(shift, queries, DOC, -2)
    offsets_far = moved(shift, offsets, DOC, -4)
    offsets_near = moved(shift, offsets, DOC, -2)
    other_keys = moved(swap, mem_keys, "core")
    other_values = moved(swap, mem_values, "core")
    near_weight = moved(part_ways, out_weight)
    own_keys, own_values, own_weight, *local = load(mem_keys, mem_values, out_weight, queries, local_keys, local_values)
    memory = (own_keys, own_values, other_keys, other_values)

    def at_home(local, half):
        def kernel(*refs):
            home_kernel(*refs, half=half)

        return attention(kernel, (offsets, mem_lengths), (*local, *memory), rows // 2, width)

    def guest(load, table, back, first, rows):
        def kernel(*refs):
            guest_kernel(*refs, back=back, first=first)

        out = attention(kernel, (table, mem_lengths), (load, *memory), rows, width)
        return out, moved(shift, out, DOC, back)

    home0 = at_home(local, 0)
    far, from_far = guest(after(query_far, home0), offsets_far, 4, 0, rows)
    query_near = after(query_near, far)
    near0, from_near0 = guest(query_near, offsets_near, 2, 0, rows // 2)

    near_weight = after(near_weight, near0)
    passed_on = pass_on(near_weight)
    far_weight = moved(part_ways, passed_on)

    near1, from_near1 = guest(after(query_near, near0, passed_on), offsets_near, 2, rows // 2, rows // 2)
    home1 = at_home((after(local[0], near1), *local[1:]), 1)
    near_weight = after(near_weight, near1)
    weights = [own_weight, near_weight, moved(swap, near_weight, "core"), far_weight, moved(swap, far_weight, "core")]

    mine, *tiles = merge((home0, home1), (from_near0, from_near1), from_far)
    tiles = mine, *(moved(shift, tile, "x", k) for k, tile in enumerate(tiles, 1))
    given = project(tiles, weights, (), 0)
    taken = swap(given, "yh")
    kept = project(tiles, weights, (), 1)
    return (kept.astype(jnp.float32) + taken.astype(jnp.float32)).astype(jnp.bfloat16)


def solution(mesh):
    split = Mesh(mesh.devices.reshape(-1, 2, 2, 2, 4), (*DOC, *HEAD))
    placed = (
        P(DOC, HEAD),
        P(DOC, HEAD),
        P(DOC, HEAD),
        P(DOC, HEAD),
        P(DOC, HEAD),
        P(DOC, None),
        P(),
        P(HEAD, None),
    )
    return jax.shard_map(step, mesh=split, in_specs=placed, out_specs=P((*DOC, *HEAD), None), check_vma=False)
```

```python
import math

import jax
import jax.numpy as jnp
from jax import lax
from jax.experimental import pallas as pl
from jax.experimental.pallas import tpu as pltpu
from jax.sharding import Mesh
from jax.sharding import PartitionSpec as P

DH = 128
DOC = ("z", "yl", "core")
HEAD = ("yh", "x")
NEG = -1e30
KEY_CHUNK = 512
TAIL = 16
SCALE = math.log2(math.e) / math.sqrt(DH)

VMEM_LIMIT = 24 * 2**20


def shift(value, axis, steps):
    count = lax.axis_size(axis)
    return lax.ppermute(value, axis, [(i, (i + steps) % count) for i in range(count)])


def return_tile(value, steps, along):
    documents, count = lax.axis_size(DOC), lax.axis_size("x")
    pairs = [
        (d * count + x, (d + steps) % documents * count + (x + along) % count)
        for d in range(documents)
        for x in range(count)
    ]
    return lax.ppermute(value, (*DOC, "x"), pairs)


def swap(value, axis):
    return lax.ppermute(value, axis, [(0, 1), (1, 0)])


def part_ways(value):
    count = lax.axis_size("x")
    up = [(i, (i + 1) % count) for i in range(count)]
    down = [(count + i, count + (i - 1) % count) for i in range(count)]
    return lax.ppermute(value, ("core", "x"), up + down)


def lanes(x, width):
    return jnp.concatenate([x] * (width // DH), axis=1)


def scores_of(q, k):
    return lax.dot_general(q, k, (((1,), (1,)), ((), ())), preferred_element_type=jnp.float32) * SCALE


def with_ones(v):
    return jnp.concatenate([v, jnp.ones(v.shape, v.dtype)], axis=1)


def absorb(h, s, v, m_ref, acc_ref):
    m_old = m_ref[h]
    m_new = jnp.maximum(m_old, jnp.max(s, axis=1, keepdims=True))
    p = jnp.exp2(s - lanes(m_new, s.shape[1])).astype(jnp.bfloat16)
    pv = jnp.dot(p, with_ones(v), preferred_element_type=jnp.float32)
    acc_ref[h] = acc_ref[h] * lanes(jnp.exp2(m_old - m_new), 2 * DH) + pv
    m_ref[h] = m_new


def reset(m_ref, acc_ref):
    m_ref[...] = jnp.full(m_ref.shape, NEG, jnp.float32)
    acc_ref[...] = jnp.zeros(acc_ref.shape, jnp.float32)


def log2_count(count):
    return jnp.where(count >= 4, 2.0, jnp.where(count >= 3, math.log2(3), jnp.where(count >= 2, 1.0, 0.0)))


def of_head(h):
    return slice(h * DH, (h + 1) * DH)


def absorb_memories(memories, lengths, counts, queries, m_ref, acc_ref):
    for (keys, values), length, count in zip(memories, lengths, counts):
        live, weight = jnp.where(count > 0, length, 0), log2_count(count)

        def fold(chunk, carry, keys=keys, values=values, live=live, weight=weight):
            start = pl.multiple_of(chunk * KEY_CHUNK, KEY_CHUNK)
            row = lax.broadcasted_iota(jnp.int32, (1, KEY_CHUNK), 1) + start
            bias = jnp.where(row < live, weight, NEG)
            for h in range(m_ref.shape[0]):
                k, v = (a[pl.ds(start, KEY_CHUNK), of_head(h)] for a in (keys, values))
                absorb(h, scores_of(queries(h), k) + bias, v, m_ref, acc_ref)
            return carry

        lax.fori_loop(0, (live + KEY_CHUNK - 1) // KEY_CHUNK, fold, 0)


def finish(out_refs, level_ref, m_ref, acc_ref):
    heads = m_ref.shape[0]
    for n, out_ref in enumerate(out_refs):
        rows = out_ref.shape[0] - TAIL
        span = slice(n * rows, (n + 1) * rows)
        level_ref[...] = jnp.zeros(level_ref.shape, jnp.float32)
        for h in range(heads):
            total = acc_ref[h, span, DH:]
            seen = total > 0
            safe = jnp.where(seen, total, 1.0)
            out_ref[:rows, of_head(h)] = (acc_ref[h, span, :DH] / safe).astype(jnp.bfloat16)
            rest = jnp.where(seen, m_ref[h, span, :] + jnp.log2(safe), NEG).T[:1, :]
            for i in range(3):
                term = rest.astype(jnp.bfloat16).astype(jnp.float32)
                level_ref[3 * h + i : 3 * h + i + 1, :rows] = term
                rest = rest - term
        out_ref[rows:, :] = level_ref[...].astype(jnp.bfloat16)


def tile_order(tiles, rows):
    count, yh = lax.axis_size("x"), lax.axis_index("yh")
    block = rows // (2 * count)
    return block, [half * (count * block) + (lax.axis_index("x") + k) % count * block for k in tiles for half in (1 - yh, yh)]


def gather(q_ref, into_ref, block, firsts):
    for n, first in enumerate(firsts):
        into_ref[n * block : (n + 1) * block, :] = q_ref[pl.ds(pl.multiple_of(first, block), block), :]


def home_kernel(offsets, lengths, q_ref, lk_ref, lv_ref, k0, v0, k1, v1, *refs, tiles):
    out_ref, m_ref, acc_ref, level_ref, rows_ref = refs
    core, document = lax.axis_index("core"), lax.axis_index(DOC)
    heads, keys = m_ref.shape[0], lk_ref.shape[0]
    count = sum(jnp.where((offsets[0, i] == 1) & (core == 1), 1, 0) for i in range(offsets.shape[1]))
    reset(m_ref, acc_ref)
    block, firsts = tile_order(tiles, q_ref.shape[0])
    gather(q_ref, rows_ref, block, firsts)

    def queries(h):
        return rows_ref[:, of_head(h)]

    row = jnp.concatenate([lax.broadcasted_iota(jnp.int32, (block, keys), 0) + first for first in firsts], axis=0)
    seen = row >= lax.broadcasted_iota(jnp.int32, row.shape, 1)
    for h in range(heads):
        s = jnp.where(seen, scores_of(queries(h), lk_ref[:, of_head(h)]), NEG)
        absorb(h, s, lv_ref[:, of_head(h)], m_ref, acc_ref)
    live = lengths[document], lengths[document + 1 - 2 * core]
    absorb_memories(((k0, v0), (k1, v1)), live, (jnp.int32(1), count), queries, m_ref, acc_ref)
    finish([out_ref], level_ref, m_ref, acc_ref)


def guest_kernel(offsets, lengths, q_ref, k0, v0, k1, v1, *refs, back):
    *out_refs, m_ref, acc_ref, level_ref, rows_ref = refs
    core, document = lax.axis_index("core"), lax.axis_index(DOC)
    reset(m_ref, acc_ref)
    gather(q_ref, rows_ref, *tile_order(range(lax.axis_size("x")), q_ref.shape[0]))
    counts = [
        sum(jnp.where(offsets[0, i] == wanted, 1, 0) for i in range(offsets.shape[1]))
        for wanted in (back, back - 1 + 2 * core)
    ]
    live = lengths[document], lengths[document + 1 - 2 * core]
    absorb_memories(((k0, v0), (k1, v1)), live, counts, lambda h: rows_ref[:, of_head(h)], m_ref, acc_ref)
    finish(out_refs, level_ref, m_ref, acc_ref)


def on_chip(value):
    return pltpu.with_memory_space_constraint(value, pltpu.VMEM)


def kernel_call(kernel, scalars, arrays, outs, scratch):
    space = pl.BlockSpec(memory_space=pltpu.VMEM)
    return pl.pallas_call(
        kernel,
        grid_spec=pltpu.PrefetchScalarGridSpec(
            num_scalar_prefetch=len(scalars),
            grid=(),
            in_specs=[space] * len(arrays),
            out_specs=[space] * len(outs),
            scratch_shapes=scratch,
        ),
        out_shape=[pltpu.VMEM(shape, jnp.bfloat16) for shape in outs],
        compiler_params=pltpu.CompilerParams(vmem_limit_bytes=VMEM_LIMIT),
    )(*scalars, *arrays)


def attention(kernel, scalars, arrays, rows, width, parts=1):
    heads = width // DH
    scratch = [
        pltpu.VMEM((heads, rows, DH), jnp.float32),
        pltpu.VMEM((heads, rows, 2 * DH), jnp.float32),
        pltpu.VMEM((TAIL, width), jnp.float32),
        pltpu.VMEM((rows, width), jnp.bfloat16),
    ]
    return kernel_call(kernel, scalars, arrays, [(rows // parts + TAIL, width)] * parts, scratch)


def load_kernel(*refs):
    *pairs, sems = refs
    count = len(pairs) // 2
    copies = [pltpu.make_async_copy(pairs[i], pairs[count + i], sems.at[i]) for i in range(count)]
    for copy in copies:
        copy.start()
    for copy in copies:
        copy.wait()


def load(*arrays):
    return pl.pallas_call(
        load_kernel,
        in_specs=[pl.BlockSpec(memory_space=pltpu.HBM)] * len(arrays),
        out_specs=[pl.BlockSpec(memory_space=pltpu.VMEM)] * len(arrays),
        out_shape=[pltpu.VMEM(a.shape, a.dtype) for a in arrays],
        scratch_shapes=[pltpu.SemaphoreType.DMA((len(arrays),))],
        compiler_params=pltpu.CompilerParams(vmem_limit_bytes=VMEM_LIMIT),
        name="load",
    )(*(pltpu.with_memory_space_constraint(a, pltpu.HBM) for a in arrays))


def pass_on_kernel(weights, half_ref):
    half = half_ref.shape[0]
    half_ref[...] = weights[pl.ds(pl.multiple_of(lax.axis_index("core") * half, half), half), :]


def pass_on(weights):
    depth, width = weights.shape
    return kernel_call(pass_on_kernel, (), (weights,), [(depth // 2, width)], [])[0]


def levels_of(part, where):
    terms = part[-TAIL:, where].astype(jnp.float32)
    return [terms[3 * h : 3 * h + 1] + terms[3 * h + 1 : 3 * h + 2] + terms[3 * h + 2 : 3 * h + 3] for h in range(TAIL // 3)]


def merged(parts, heads, share_ref):
    levels = [levels_of(part, where) for part, where in parts]
    joint = []
    for h in range(heads):
        a, b = levels[0][h], levels[1][h]
        top = jnp.maximum(a, b)
        shares = jnp.exp2(a - top), jnp.exp2(b - top)
        total = shares[0] + shares[1]
        joint.append(top + jnp.log2(total))
        for i, share in enumerate(shares):
            share_ref[2 * h + i : 2 * h + i + 1, :] = share / total
    columns = share_ref[...].T
    rows = [
        sum(columns[:, 2 * h + i : 2 * h + i + 1] * part[where, of_head(h)].astype(jnp.float32) for i, (part, where) in enumerate(parts))
        for h in range(heads)
    ]
    return rows, joint


def premerge_kernel(home0, home1, far_ref, *refs):
    *tiles, share_ref, level_ref = refs
    heads = far_ref.shape[1] // DH
    for k, tile in enumerate(tiles):
        rows = tile.shape[0] - TAIL
        home = (home0, home1)[k // 2]
        parts = [(home, pl.ds(k % 2 * rows, rows)), (far_ref, pl.ds(k * rows, rows))]
        merged_rows, joint = merged(parts, heads, share_ref)
        level_ref[...] = jnp.zeros(level_ref.shape, jnp.float32)
        for h in range(heads):
            tile[:rows, of_head(h)] = merged_rows[h].astype(jnp.bfloat16)
            rest = joint[h]
            for i in range(3):
                term = rest.astype(jnp.bfloat16).astype(jnp.float32)
                level_ref[3 * h + i : 3 * h + i + 1, :rows] = term
                rest = rest - term
        tile[rows:, :] = level_ref[...].astype(jnp.bfloat16)


def premerge(home0, home1, far):
    width = far.shape[1]
    count = lax.axis_size("x")
    rows = (far.shape[0] - TAIL) // count
    scratch = [pltpu.VMEM((DH, rows), jnp.float32), pltpu.VMEM((TAIL, width), jnp.float32)]
    return kernel_call(premerge_kernel, (), (home0, home1, far), [(rows + TAIL, width)] * count, scratch)


def project_kernel(*refs, part):
    own, near, near_other, far, far_other, out_ref, share_ref, row_ref = refs[8:]
    tiles = list(zip(refs[:4], refs[4:8]))
    half, core, heads = far.shape[0], lax.axis_index("core"), own.shape[0] // DH
    rows = out_ref.shape[0]
    for n, pair in enumerate(tiles):
        mixed, _ = merged([(ref, pl.ds(0, 2 * rows)) for ref in pair], heads, share_ref)
        for h in range(heads):
            row_ref[n, :, of_head(h)] = mixed[h][part * rows : (part + 1) * rows].astype(jnp.bfloat16)
    below, above = row_ref[1], row_ref[3]
    pairs = [
        (row_ref[0], own),
        (jnp.where(core == 0, below, above), near),
        (jnp.where(core == 0, above, below), near_other),
        (jnp.where(core == 0, row_ref[2, :, :half], row_ref[2, :, half:]), far),
        (jnp.where(core == 0, row_ref[2, :, half:], row_ref[2, :, :half]), far_other),
    ]
    acc = sum(jnp.dot(a, w[...], preferred_element_type=jnp.float32) for a, w in pairs)
    out_ref[...] = acc.astype(out_ref.dtype)


def project(tiles, nears, weights, part):
    def kernel(*refs):
        project_kernel(*refs, part=part)

    depth, width = weights[0].shape
    rows = (tiles[0].shape[0] - TAIL) // 2
    scratch = [pltpu.VMEM((DH, 2 * rows), jnp.float32), pltpu.VMEM((len(tiles), rows, depth), jnp.bfloat16)]
    return kernel_call(kernel, (), (*tiles, *nears, *weights), [(rows, width)], scratch)[0]


def after(value, *others):
    return lax.optimization_barrier((value, *others))[0]


def step(queries, local_keys, local_values, mem_keys, mem_values, offsets, mem_lengths, out_weight):
    rows, width = queries.shape

    def moved(move, value, *where):
        value = move(value, *where)
        return on_chip(value) if value.dtype == jnp.bfloat16 else value

    query_far = moved(shift, queries, DOC, -4)
    query_near = moved(shift, queries, DOC, -2)
    offsets_far = moved(shift, offsets, DOC, -4)
    offsets_near = moved(shift, offsets, DOC, -2)
    other_keys = moved(swap, mem_keys, "core")
    other_values = moved(swap, mem_values, "core")
    near_weight = moved(part_ways, out_weight)
    own_keys, own_values, own_weight, *local = load(mem_keys, mem_values, out_weight, queries, local_keys, local_values)
    memory = (own_keys, own_values, other_keys, other_values)

    count = lax.axis_size("x")

    def at_home(local, half):
        def kernel(*refs):
            home_kernel(*refs, tiles=range(half * count // 2, (half + 1) * count // 2))

        return attention(kernel, (offsets, mem_lengths), (*local, *memory), rows // 2, width)[0]

    def guest(load, table, back, parts):
        def kernel(*refs):
            guest_kernel(*refs, back=back)

        return attention(kernel, (table, mem_lengths), (load, *memory), rows, width, parts)

    home0 = at_home(local, 0)
    (far,) = guest(after(query_far, home0), offsets_far, 4, 1)
    from_far = moved(shift, far, DOC, 4)

    near_weight = after(near_weight, far)
    passed_on = pass_on(near_weight)
    far_weight = moved(part_ways, passed_on)
    weights = [own_weight, near_weight, moved(swap, near_weight, "core"), far_weight, moved(swap, far_weight, "core")]

    near = guest(after(query_near, far, passed_on), offsets_near, 2, count)
    nears = [moved(return_tile, tile, 2, k) for k, tile in enumerate(near)]
    home1 = at_home((after(local[0], *near), *local[1:]), 1)
    mine, *tiles = premerge(home0, home1, from_far)
    tiles = mine, *(moved(shift, tile, "x", k) for k, tile in enumerate(tiles, 1))
    given = project(tiles, nears, weights, 0)
    taken = swap(given, "yh")
    kept = project(tiles, nears, weights, 1)
    return (kept.astype(jnp.float32) + taken.astype(jnp.float32)).astype(jnp.bfloat16)


def solution(mesh):
    split = Mesh(mesh.devices.reshape(-1, 2, 2, 2, 4), (*DOC, *HEAD))
    placed = (
        P(DOC, HEAD),
        P(DOC, HEAD),
        P(DOC, HEAD),
        P(DOC, HEAD),
        P(DOC, HEAD),
        P(DOC, None),
        P(),
        P(HEAD, None),
    )
    return jax.shard_map(step, mesh=split, in_specs=placed, out_specs=P((*DOC, *HEAD), None), check_vma=False)
```

```python
import math

import jax
import jax.numpy as jnp
from jax import lax
from jax.experimental import pallas as pl
from jax.experimental.pallas import tpu as pltpu
from jax.sharding import Mesh
from jax.sharding import PartitionSpec as P

DH = 128
DOC = ("z", "yl", "core")
HEAD = ("yh", "x")
NEG = -1e30
KEY_CHUNK = 512
TAIL = 16
SCALE = math.log2(math.e) / math.sqrt(DH)

VMEM_LIMIT = 24 * 2**20


def shift(value, axis, steps):
    count = lax.axis_size(axis)
    return lax.ppermute(value, axis, [(i, (i + steps) % count) for i in range(count)])


def swap(value, axis):
    return lax.ppermute(value, axis, [(0, 1), (1, 0)])


def part_ways(value):
    count = lax.axis_size("x")
    up = [(i, (i + 1) % count) for i in range(count)]
    down = [(count + i, count + (i - 1) % count) for i in range(count)]
    return lax.ppermute(value, ("core", "x"), up + down)


def lanes(x, width):
    return jnp.concatenate([x] * (width // DH), axis=1)


def scores_of(q, k):
    return lax.dot_general(q, k, (((1,), (1,)), ((), ())), preferred_element_type=jnp.float32) * SCALE


def with_ones(v):
    return jnp.concatenate([v, jnp.ones(v.shape, v.dtype)], axis=1)


def absorb(h, s, v, m_ref, acc_ref):
    m_old = m_ref[h]
    m_new = jnp.maximum(m_old, jnp.max(s, axis=1, keepdims=True))
    p = jnp.exp2(s - lanes(m_new, s.shape[1])).astype(jnp.bfloat16)
    pv = jnp.dot(p, with_ones(v), preferred_element_type=jnp.float32)
    acc_ref[h] = acc_ref[h] * lanes(jnp.exp2(m_old - m_new), 2 * DH) + pv
    m_ref[h] = m_new


def reset(m_ref, acc_ref):
    m_ref[...] = jnp.full(m_ref.shape, NEG, jnp.float32)
    acc_ref[...] = jnp.zeros(acc_ref.shape, jnp.float32)


def log2_count(count):
    return jnp.where(count >= 4, 2.0, jnp.where(count >= 3, math.log2(3), jnp.where(count >= 2, 1.0, 0.0)))


def of_head(h):
    return slice(h * DH, (h + 1) * DH)


def absorb_memories(memories, lengths, counts, queries, m_ref, acc_ref):
    for (keys, values), length, count in zip(memories, lengths, counts):
        live, weight = jnp.where(count > 0, length, 0), log2_count(count)

        def fold(chunk, carry, keys=keys, values=values, live=live, weight=weight):
            start = pl.multiple_of(chunk * KEY_CHUNK, KEY_CHUNK)
            row = lax.broadcasted_iota(jnp.int32, (1, KEY_CHUNK), 1) + start
            bias = jnp.where(row < live, weight, NEG)
            for h in range(m_ref.shape[0]):
                k, v = (a[pl.ds(start, KEY_CHUNK), of_head(h)] for a in (keys, values))
                absorb(h, scores_of(queries(h), k) + bias, v, m_ref, acc_ref)
            return carry

        lax.fori_loop(0, (live + KEY_CHUNK - 1) // KEY_CHUNK, fold, 0)


def finish(out_ref, level_ref, m_ref, acc_ref):
    heads, rows = m_ref.shape[:2]
    level_ref[...] = jnp.zeros(level_ref.shape, jnp.float32)
    for h in range(heads):
        total = acc_ref[h, :, DH:]
        seen = total > 0
        safe = jnp.where(seen, total, 1.0)
        out_ref[:rows, of_head(h)] = (acc_ref[h, :, :DH] / safe).astype(jnp.bfloat16)
        rest = jnp.where(seen, m_ref[h] + jnp.log2(safe), NEG).T[:1, :]
        for i in range(3):
            term = rest.astype(jnp.bfloat16).astype(jnp.float32)
            level_ref[3 * h + i : 3 * h + i + 1, :rows] = term
            rest = rest - term
    out_ref[rows:, :] = level_ref[...].astype(jnp.bfloat16)


def home_kernel(offsets, lengths, q_ref, lk_ref, lv_ref, k0, v0, k1, v1, out_ref, m_ref, acc_ref, level_ref, *, half):
    core, document = lax.axis_index("core"), lax.axis_index(DOC)
    heads, rows = m_ref.shape[:2]
    first, keys = half * rows, (half + 1) * rows
    count = sum(jnp.where((offsets[0, i] == 1) & (core == 1), 1, 0) for i in range(offsets.shape[1]))
    reset(m_ref, acc_ref)

    def queries(h):
        return q_ref[first : first + rows, of_head(h)]

    seen = lax.broadcasted_iota(jnp.int32, (rows, keys), 0) + first >= lax.broadcasted_iota(jnp.int32, (rows, keys), 1)
    for h in range(heads):
        s = jnp.where(seen, scores_of(queries(h), lk_ref[:keys, of_head(h)]), NEG)
        absorb(h, s, lv_ref[:keys, of_head(h)], m_ref, acc_ref)
    live = lengths[document], lengths[document + 1 - 2 * core]
    absorb_memories(((k0, v0), (k1, v1)), live, (jnp.int32(1), count), queries, m_ref, acc_ref)
    finish(out_ref, level_ref, m_ref, acc_ref)


def guest_kernel(offsets, lengths, q_ref, k0, v0, k1, v1, *refs, back):
    out_ref, m_ref, acc_ref, level_ref = refs
    core, document = lax.axis_index("core"), lax.axis_index(DOC)
    reset(m_ref, acc_ref)
    counts = [
        sum(jnp.where(offsets[0, i] == wanted, 1, 0) for i in range(offsets.shape[1]))
        for wanted in (back, back - 1 + 2 * core)
    ]
    live = lengths[document], lengths[document + 1 - 2 * core]
    absorb_memories(((k0, v0), (k1, v1)), live, counts, lambda h: q_ref[:, of_head(h)], m_ref, acc_ref)
    finish(out_ref, level_ref, m_ref, acc_ref)


def on_chip(value):
    return pltpu.with_memory_space_constraint(value, pltpu.VMEM)


def kernel_call(kernel, scalars, arrays, outs, scratch):
    space = pl.BlockSpec(memory_space=pltpu.VMEM)
    return pl.pallas_call(
        kernel,
        grid_spec=pltpu.PrefetchScalarGridSpec(
            num_scalar_prefetch=len(scalars),
            grid=(),
            in_specs=[space] * len(arrays),
            out_specs=[space] * len(outs),
            scratch_shapes=scratch,
        ),
        out_shape=[pltpu.VMEM(shape, jnp.bfloat16) for shape in outs],
        compiler_params=pltpu.CompilerParams(vmem_limit_bytes=VMEM_LIMIT),
    )(*scalars, *arrays)


def attention(kernel, scalars, arrays, rows, width):
    heads = width // DH
    scratch = [
        pltpu.VMEM((heads, rows, DH), jnp.float32),
        pltpu.VMEM((heads, rows, 2 * DH), jnp.float32),
        pltpu.VMEM((TAIL, width), jnp.float32),
    ]
    return kernel_call(kernel, scalars, arrays, [(rows + TAIL, width)], scratch)[0]


def load_kernel(*refs):
    *pairs, sems = refs
    count = len(pairs) // 2
    copies = [pltpu.make_async_copy(pairs[i], pairs[count + i], sems.at[i]) for i in range(count)]
    for copy in copies:
        copy.start()
    for copy in copies:
        copy.wait()


def load(*arrays):
    return pl.pallas_call(
        load_kernel,
        in_specs=[pl.BlockSpec(memory_space=pltpu.HBM)] * len(arrays),
        out_specs=[pl.BlockSpec(memory_space=pltpu.VMEM)] * len(arrays),
        out_shape=[pltpu.VMEM(a.shape, a.dtype) for a in arrays],
        scratch_shapes=[pltpu.SemaphoreType.DMA((len(arrays),))],
        compiler_params=pltpu.CompilerParams(vmem_limit_bytes=VMEM_LIMIT),
        name="load",
    )(*(pltpu.with_memory_space_constraint(a, pltpu.HBM) for a in arrays))


def pass_on_kernel(weights, half_ref):
    half = half_ref.shape[0]
    half_ref[...] = weights[pl.ds(pl.multiple_of(lax.axis_index("core") * half, half), half), :]


def pass_on(weights):
    depth, width = weights.shape
    return kernel_call(pass_on_kernel, (), (weights,), [(depth // 2, width)], [])[0]


def merge_kernel(*refs):
    *homes, far_ref, near_ref = refs[:4]
    *tiles, share_ref, whole_ref = refs[4:]
    rows, width = whole_ref.shape
    heads, count = width // DH, len(tiles)
    half = rows // 2
    for n, home_ref in enumerate(homes):
        span = slice(n * half, (n + 1) * half)
        parts = [(home_ref, slice(0, half)), (far_ref, span), (near_ref, span)]
        tails = [part[-TAIL:, where].astype(jnp.float32) for part, where in parts]
        for h in range(heads):
            levels = [tail[3 * h : 3 * h + 1] + tail[3 * h + 1 : 3 * h + 2] + tail[3 * h + 2 : 3 * h + 3] for tail in tails]
            top = jnp.maximum(jnp.maximum(levels[0], levels[1]), levels[2])
            shares = [jnp.exp2(level - top) for level in levels]
            total = shares[0] + shares[1] + shares[2]
            for i, share in enumerate(shares):
                share_ref[n, 3 * h + i : 3 * h + i + 1, :] = share / total
        columns = share_ref[n].T
        for h in range(heads):
            mixed = 0.0
            for i, (part, where) in enumerate(parts):
                mixed = mixed + columns[:, 3 * h + i : 3 * h + i + 1] * part[where, of_head(h)].astype(jnp.float32)
            whole_ref[span, of_head(h)] = mixed.astype(whole_ref.dtype)
    block = half // count
    x, yh = lax.axis_index("x"), lax.axis_index("yh")
    for k, tile in enumerate(tiles):
        for n, side in enumerate((1 - yh, yh)):
            first = side * half + (x + k) % count * block
            tile[n * block : (n + 1) * block, :] = whole_ref[pl.ds(pl.multiple_of(first, block), block), :]


def merge(home0, home1, far, near):
    rows, width = far.shape[0] - TAIL, far.shape[1]
    count = lax.axis_size("x")
    scratch = [pltpu.VMEM((2, DH, rows // 2), jnp.float32), pltpu.VMEM((rows, width), jnp.bfloat16)]
    return kernel_call(merge_kernel, (), (home0, home1, far, near), [(rows // count, width)] * count, scratch)


def project_kernel(*refs, part):
    mine, below, opposite, above, own, near, near_other, far, far_other, *extra, out_ref = refs
    rows, half = out_ref.shape[0], far.shape[0]
    core = lax.axis_index("core")

    def tile(ref):
        return ref[part * rows : (part + 1) * rows, :]

    pairs = [
        (tile(mine), own),
        (jnp.where(core == 0, tile(below), tile(above)), near),
        (jnp.where(core == 0, tile(above), tile(below)), near_other),
        (jnp.where(core == 0, tile(opposite)[:, :half], tile(opposite)[:, half:]), far),
        (jnp.where(core == 0, tile(opposite)[:, half:], tile(opposite)[:, :half]), far_other),
    ]
    acc = sum(jnp.dot(a, w[...], preferred_element_type=jnp.float32) for a, w in pairs)
    for ref in extra:
        acc = acc + ref[...].astype(jnp.float32)
    out_ref[...] = acc.astype(out_ref.dtype)


def project(tiles, weights, extra, part):
    def kernel(*refs):
        project_kernel(*refs, part=part)

    out = (tiles[0].shape[0] // 2, weights[0].shape[1])
    return kernel_call(kernel, (), (*tiles, *weights, *extra), [out], [])[0]


def after(value, *others):
    return lax.optimization_barrier((value, *others))[0]


def step(queries, local_keys, local_values, mem_keys, mem_values, offsets, mem_lengths, out_weight):
    rows, width = queries.shape

    def moved(move, value, *where):
        value = move(value, *where)
        return on_chip(value) if value.dtype == jnp.bfloat16 else value

    query_far = moved(shift, queries, DOC, -4)
    query_near = moved(shift, queries, DOC, -2)
    offsets_far = moved(shift, offsets, DOC, -4)
    offsets_near = moved(shift, offsets, DOC, -2)
    other_keys = moved(swap, mem_keys, "core")
    other_values = moved(swap, mem_values, "core")
    near_weight = moved(part_ways, out_weight)
    own_keys, own_values, own_weight, *local = load(mem_keys, mem_values, out_weight, queries, local_keys, local_values)
    memory = (own_keys, own_values, other_keys, other_values)

    def at_home(local, half):
        def kernel(*refs):
            home_kernel(*refs, half=half)

        return attention(kernel, (offsets, mem_lengths), (*local, *memory), rows // 2, width)

    def guest(load, table, back):
        def kernel(*refs):
            guest_kernel(*refs, back=back)

        out = attention(kernel, (table, mem_lengths), (load, *memory), rows, width)
        return moved(shift, out, DOC, back), out

    home0 = at_home(local, 0)
    from_far, far = guest(after(query_far, home0), offsets_far, 4)

    near_weight = after(near_weight, far)
    passed_on = pass_on(near_weight)
    far_weight = moved(part_ways, passed_on)

    from_near, near = guest(after(query_near, far, passed_on), offsets_near, 2)
    home1 = at_home((after(local[0], near), *local[1:]), 1)
    far_weight = after(far_weight, home1)
    weights = [own_weight, near_weight, moved(swap, near_weight, "core"), far_weight, moved(swap, far_weight, "core")]

    mine, *tiles = merge(home0, home1, from_far, from_near)
    tiles = mine, *(moved(shift, tile, "x", k) for k, tile in enumerate(tiles, 1))
    given = project(tiles, weights, (), 0)
    taken = swap(given, "yh")
    kept = project(tiles, weights, (), 1)
    return (kept.astype(jnp.float32) + taken.astype(jnp.float32)).astype(jnp.bfloat16)


def solution(mesh):
    split = Mesh(mesh.devices.reshape(-1, 2, 2, 2, 4), (*DOC, *HEAD))
    placed = (
        P(DOC, HEAD),
        P(DOC, HEAD),
        P(DOC, HEAD),
        P(DOC, HEAD),
        P(DOC, HEAD),
        P(DOC, None),
        P(),
        P(HEAD, None),
    )
    return jax.shard_map(step, mesh=split, in_specs=placed, out_specs=P((*DOC, *HEAD), None), check_vma=False)
```
